512 devices in a mesh: seq: 64 (over z, x, core), mp: 8 (over y).
Axes of the slice: x: 4, y: 8, z: 8, core: 2. Of those that a mesh axis runs over, the one named last changes fastest.
Arguments:
- tokens: bfloat16 [32768, 1792], P('seq'), may hold values from -400 to 400, as said below
- norm_gain: float32 [1792], replicated, may hold values from 0.1 to 1.9
- q_weight: bfloat16 [1792, 256], P(None, 'mp'), may hold values from -0.125 to 0.125
- k_weight: bfloat16 [1792, 256], P(None, 'mp'), may hold values from -0.125 to 0.125
- v_weight: bfloat16 [1792, 1792], P(None, 'mp'), may hold values from -0.125 to 0.125
- out_gain: float32 [1792], P('mp'), may hold values from 0.1 to 1.9
- o_weight: bfloat16 [1792, 1792], P('mp'), may hold values from -0.125 to 0.125
- lengths: int32 [8], replicated, may hold values from 1 to 16384, 32768 in all
Outputs:
- mixed: bfloat16 [32768, 1792], P('seq', 'mp')
The draws below stay inside these ranges and needn't reach their ends.
Inputs may be any that keep to these rules, and one draw needn't show every extreme that they name: The lengths sum to 32768; the longest is exactly 16384. `tokens`: finite hidden states.
All inputs are finite; a program needn't handle non-finite values.
Results may differ from the reference program's by a relative error of at most 0.02.
Values may be sent and summed in bfloat16 or wider, within the bound.
A program may use at most 64 MiB of HBM per device.

```python
import math
import jax
import jax.numpy as jnp
import numpy as np
from jax import lax

D = 1792
H = 16
FEAT = 16
VDIM = 112
TERMS = 273
TOK_DEV = 512
REQS = 8
TOKENS = 32768
LONGEST = 16384


def draw_tokens(key, part):
    key_base = jax.random.fold_in(key, 11)
    key_rows = jax.random.fold_in(key, 12)
    key_cols = jax.random.fold_in(key, 13)
    base_values = jnp.clip(jax.random.normal(key_base, (TOKENS, D), jnp.float32), -4.0, 4.0)
    row_scale = jnp.exp(jax.random.uniform(key_rows, (TOKENS, 1), jnp.float32, 0.0, math.log(10.0)))
    col_scale = jnp.exp(jax.random.uniform(key_cols, (1, D), jnp.float32, 0.0, math.log(10.0)))
    return (base_values * row_scale * col_scale).astype(jnp.bfloat16)


def steps_of(own_key, dims, shards, smallest, high):
    loudness, own = 1.0, jax.random.fold_in(own_key, 6)
    for dim, shards_of in shards:
        draws = jnp.exp(jax.random.uniform(jax.random.fold_in(own, dim), (shards_of,), jnp.float32, smallest / len(shards), high / len(shards)))
        loudness = loudness * jnp.repeat(draws, dims[dim] // shards_of).reshape([-1 if axis == dim else 1 for axis in range(len(dims))])
    return loudness


def profile(count, total, bound, slope):
    portions = [(1 << 20) // math.isqrt(rank ** slope) + 1 for rank in range(2, count + 1)]
    spare, counts = total - bound - (count - 1), [1] * (count - 1)
    while spare > 0:
        candidates = [i for i in range(count - 1) if counts[i] < bound]
        whole, left = sum([portions[i] for i in candidates]), spare
        for i in candidates:
            addition = min(bound - counts[i], max(1, left * portions[i] // whole), spare)
            counts[i] = counts[i] + addition
            spare = spare - addition
    return np.array([bound] + counts)


def ragged_sizes(own_key, number_of, total, bound, slope):
    if number_of == 2:
        one = jax.random.randint(own_key, (), max(1, total - bound), min(bound, total - 1) + 1)
        return jnp.stack([one, total - one])
    sizes = jnp.asarray(profile(number_of, total, bound, slope), jnp.int32)
    twos = (number_of - 1) // 2
    source_of, sink = sizes[1:1 + 2 * twos:2], sizes[2:2 + 2 * twos:2]
    margin = jnp.minimum(source_of - 1, bound - sink)
    passed = jax.random.randint(jax.random.fold_in(own_key, 1), (twos,), 0, 1 << 20) % (margin + 1)
    sizes = sizes.at[1:1 + 2 * twos:2].set(source_of - passed).at[2:2 + 2 * twos:2].set(sink + passed)
    return sizes[jax.random.permutation(jax.random.fold_in(own_key, 2), number_of)]


def normal_values(rng, shape, spread, limit, cuts=(), held_as=jnp.bfloat16):
    level = steps_of(rng, shape, cuts, -0.22, 0.18) if cuts else 1.0
    result = jax.random.normal(rng, shape, jnp.float32) * spread * level
    return jnp.minimum(jnp.maximum(result, -limit), limit).astype(held_as)


def setup_inputs(seed: int = 0) -> dict:
    keys = jax.random.split(jax.random.key(seed), 9)
    tokens = draw_tokens(jax.random.fold_in(keys[8], 71), 0)
    norm_gain = jnp.clip(1.0 + 0.18 * jax.random.normal(keys[1], (D,), jnp.float32), 0.1, 1.9)
    q_weight = normal_values(keys[2], (D, H * FEAT), D ** -0.5, 0.125, ((1, 8),))
    k_weight = normal_values(keys[3], (D, H * FEAT), D ** -0.5, 0.125, ((1, 8),))
    v_weight = normal_values(keys[4], (D, D), D ** -0.5, 0.125, ((1, 8),))
    out_gain = jnp.clip(1.0 + 0.18 * jax.random.normal(keys[5], (D,), jnp.float32), 0.1, 1.9)
    o_weight = normal_values(keys[6], (D, D), D ** -0.5, 0.125, ((0, 8),))
    lengths = ragged_sizes(keys[7], REQS, TOKENS, LONGEST, 2).astype(jnp.int32)
    return dict(tokens=tokens, norm_gain=norm_gain, q_weight=q_weight, k_weight=k_weight, v_weight=v_weight, out_gain=out_gain, o_weight=o_weight, lengths=lengths)


def doc_starts(positions, lengths):
    doc_ends = jnp.cumsum(lengths).astype(jnp.int32)
    finished = doc_ends[None, :] <= positions[:, None]
    return lax.optimization_barrier(jnp.sum(jnp.where(finished, lengths[None, :], 0), axis=1)).astype(jnp.int32)

def rms_norm(rows_in, gain_vec):
    widened = rows_in.astype(jnp.float32)
    row_scale = lax.rsqrt(lax.optimization_barrier(jnp.mean(widened * widened, axis=-1, keepdims=True)) + 1e-06)
    return widened * row_scale * gain_vec

def features(projected, head_count):
    row_count = projected.shape[0]
    feat_width = projected.shape[1] // head_count
    split_proj = projected.reshape(row_count, head_count, feat_width)
    linear_part = split_proj * feat_width ** (-0.25)
    square_part = (split_proj[..., :, None] * split_proj[..., None, :]).reshape(row_count, head_count, feat_width * feat_width)
    square_part = square_part * (1.0 / (math.sqrt(2.0) * math.sqrt(feat_width)))
    constant = jnp.ones((row_count, head_count, 1), split_proj.dtype)
    return jnp.concatenate([constant, linear_part, square_part], axis=-1).astype(jnp.bfloat16)

def head_gain(attended, gain_vec):
    head_count, head_width = (attended.shape[1], attended.shape[2])
    return attended * gain_vec.reshape(head_count, head_width)

def local_terms(query_feats, key_feats, values, starts, first_row):
    row_count = starts.shape[0]
    wide_query = query_feats.astype(jnp.float32)
    wide_key = key_feats.astype(jnp.float32)
    wide_values = values.astype(jnp.float32)
    scores = jnp.einsum('thf,shf->hts', wide_query, wide_key, precision=lax.Precision.HIGHEST)
    position = jnp.arange(row_count)
    kept_mask = (position[None, :] <= position[:, None]) & (starts[None, :] == starts[:, None])
    scores = jnp.where(kept_mask[None], scores, jnp.zeros_like(scores))
    scores_low = lax.optimization_barrier(scores.astype(jnp.bfloat16)).astype(jnp.float32)
    numerator = jnp.einsum('hts,shd->thd', scores_low, wide_values, precision=lax.Precision.HIGHEST)
    denominator = jnp.transpose(lax.optimization_barrier(jnp.sum(scores, axis=2)))
    in_last_doc = starts == starts[row_count - 1]
    masked_keys = jnp.where(in_last_doc[:, None, None], wide_key, jnp.zeros_like(wide_key))
    own_state = jnp.einsum('shf,shd->hfd', masked_keys, wide_values, precision=lax.Precision.HIGHEST)
    own_sum = lax.optimization_barrier(jnp.sum(masked_keys, axis=0))
    resets = (starts[row_count - 1] >= first_row).astype(jnp.float32)
    return (numerator, denominator, own_state, own_sum, resets)

def far_terms(query_feats, incoming, incoming_sum, from_before):
    widened = query_feats.astype(jnp.float32)
    far_numerator = jnp.einsum('thf,hfd->thd', widened, incoming, precision=lax.Precision.HIGHEST)
    far_denominator = jnp.einsum('thf,hf->th', widened, incoming_sum, precision=lax.Precision.HIGHEST)
    return (far_numerator * from_before[:, None, None], far_denominator * from_before[:, None])

def reference(tokens, norm_gain, q_weight, k_weight, v_weight, out_gain, o_weight, lengths):
    total_rows = tokens.shape[0]
    normed = rms_norm(tokens, norm_gain).astype(jnp.bfloat16)
    query_feats = features(jnp.dot(normed, q_weight, preferred_element_type=jnp.float32), H)
    key_feats = features(jnp.dot(normed, k_weight, preferred_element_type=jnp.float32), H)
    values = jnp.dot(normed, v_weight, preferred_element_type=jnp.float32).astype(jnp.bfloat16).reshape(total_rows, H, VDIM)
    starts = doc_starts(jnp.arange(total_rows, dtype=jnp.int32), lengths)
    block_count = total_rows // TOK_DEV

    def advance(carried, block_index):
        incoming, incoming_sum = carried
        first_row = (block_index * TOK_DEV).astype(jnp.int32)
        block_query = lax.dynamic_slice_in_dim(query_feats, first_row, TOK_DEV, 0)
        block_key = lax.dynamic_slice_in_dim(key_feats, first_row, TOK_DEV, 0)
        block_values = lax.dynamic_slice_in_dim(values, first_row, TOK_DEV, 0)
        block_starts = lax.dynamic_slice_in_dim(starts, first_row, TOK_DEV, 0)
        numerator, denominator, own_state, own_sum, resets = local_terms(block_query, block_key, block_values, block_starts, first_row)
        from_before = (block_starts < first_row).astype(jnp.float32)
        far_numerator, far_denominator = far_terms(block_query, incoming, incoming_sum, from_before)
        attended = (numerator + far_numerator) / (denominator + far_denominator)[:, :, None]
        kept = 1.0 - resets
        return ((own_state + kept * incoming, own_sum + kept * incoming_sum), attended)
    initial = (jnp.zeros((H, TERMS, VDIM), jnp.float32), jnp.zeros((H, TERMS), jnp.float32))
    _, attended = lax.scan(advance, initial, jnp.arange(block_count, dtype=jnp.int32))
    attended = attended.reshape(total_rows, H, VDIM)
    headed = head_gain(attended, out_gain).reshape(total_rows, H * VDIM).astype(jnp.bfloat16)
    return jnp.dot(headed, o_weight, preferred_element_type=jnp.float32).astype(jnp.bfloat16)
```

```python
import functools

import jax
import jax.numpy as jnp
from jax import lax
from jax.experimental import pallas as pl
from jax.experimental.pallas import tpu as pltpu
from jax.sharding import PartitionSpec as P

MESH = pl.DeviceIdType.MESH
F32, BF16, I32 = jnp.float32, jnp.bfloat16, jnp.int32

FEAT = 16
VDIM = 112
HEADS = 2
PLANE = 8
PLANES = 8
RING = 8
TERMS = 192
CHUNK = HEADS * TERMS // PLANE
VROWS = 128

RIGHTWARD = ((4, 0), (3, 1), (3, 0), (2, 1), (2, 0), (1, 1), (1, 0))
LEFTWARD = tuple((hops, 1 - half) for hops, half in RIGHTWARD)


def dot(a, b, dims):
    return lax.dot_general(a, b, (dims, ((), ())), preferred_element_type=F32)


def write_features(out, head, u, coefficients, keep):
    square, cross, linear, constant = coefficients
    for d in range(FEAT // 2 + 1):
        turned = u if d == 0 else pltpu.roll(u, d, 0)
        scale = square if d in (0, FEAT // 2) else cross
        rows = u * turned
        if scale != 1.0:
            rows = rows * scale
        if keep is not None:
            rows = rows * keep
        out[head, d * FEAT : (d + 1) * FEAT, :] = rows.astype(BF16)
    base = (FEAT // 2 + 1) * FEAT
    rows = u * linear if linear != 1.0 else u
    if keep is not None:
        rows = rows * keep
    out[head, base : base + FEAT, :] = rows.astype(BF16)
    index = lax.broadcasted_iota(I32, (2 * FEAT, u.shape[1]), 0)
    rows = jnp.where(index == 0, constant, 0.0)
    if keep is not None:
        rows = rows * keep
    out[head, base + FEAT : base + 3 * FEAT, :] = rows.astype(BF16)


def kernel(
    tok_hbm, ng_ref, wq_hbm, wk_hbm, wv_hbm, og_ref, ow_hbm, len_ref,
    out_ref,
    tok, wq, wk, wv, ow, wcat, ot, gcol,
    vt, qt, kt, knat, qs, fk, fq, num, ht,
    st, c1, ts, c2, rs, sin, send_r, send_l, recv_r, recv_l,
    load_sem, s1, r1, s2, r2, s3, r3, ssr, rsr, ssl, rsl,
):
    rows, width = tok.shape
    half_rows = rows // 2
    seq, mp = lax.axis_index("seq"), lax.axis_index("mp")
    z, p = lax.div(seq, PLANE), lax.rem(seq, PLANE)
    first_row = seq * rows

    def in_plane(r):
        return lax.rem(p + r, PLANE)

    def along_z(r):
        return lax.rem(z + r, PLANES)

    def along_mp(r):
        return lax.rem(mp + r + RING, RING)

    barrier = pltpu.get_barrier_semaphore()
    partners = [(z * PLANE + in_plane(r), mp) for r in range(1, PLANE)]
    partners += [(along_z(r) * PLANE + p, mp) for r in range(1, PLANES)]
    partners += [(seq, along_mp(1)), (seq, along_mp(-1))]
    for who in partners:
        pl.semaphore_signal(barrier, inc=1, device_id=who, device_id_type=MESH)

    steps = 4
    step_rows = rows // steps
    loads = []
    for i, (src, dst) in enumerate(((wv_hbm, wv), (wq_hbm, wq), (wk_hbm, wk))):
        loads.append(pltpu.make_async_copy(src, dst, load_sem.at[i]))
    tok_loads = [
        pltpu.make_async_copy(
            tok_hbm.at[pl.ds(i * step_rows, step_rows), :],
            tok.at[pl.ds(i * step_rows, step_rows), :],
            load_sem.at[4 + i],
        )
        for i in range(steps)
    ]
    ow_load = pltpu.make_async_copy(ow_hbm, ow, load_sem.at[3])
    for c in loads + tok_loads + [ow_load]:
        c.start()

    lens = [len_ref[i] for i in range(len_ref.shape[0])]
    ends, total = [], None
    for n in lens:
        total = n if total is None else total + n
        ends.append(total)

    def start_of(position):
        found = 0
        for n, e in zip(lens, ends):
            found = found + jnp.where(e <= position, n, 0)
        return found

    pos_row = first_row + lax.broadcasted_iota(I32, (1, rows), 1)
    starts_row = start_of(pos_row)
    low_row = starts_row - first_row
    last_start = start_of(first_row + rows - 1)
    in_last = jnp.where(pos_row >= last_start, 1.0, 0.0).astype(F32)
    from_before = jnp.where(starts_row < first_row, 1.0, 0.0).astype(F32)

    def kept(row0, count):
        goes_on = start_of(row0 + count - 1) < row0
        return jnp.where(goes_on, 1.0, 0.0).astype(F32)

    plane_rows = PLANE * rows
    keep_p = [kept(z * plane_rows + i * rows, rows) for i in range(PLANE)]
    keep_z = [kept(i * plane_rows, plane_rows) for i in range(PLANES)]

    index = lax.broadcasted_iota(I32, (VROWS - VDIM, rows), 0)
    ones = jnp.where(index == 0, 1.0, 0.0).astype(BF16)
    for h in range(HEADS):
        vt[h, VDIM:VROWS, :] = ones
    gain_row = og_ref[...].reshape(1, HEADS * VDIM)
    gcol[...] = jnp.broadcast_to(gain_row, (128, HEADS * VDIM)).T

    for c in loads:
        c.wait()
    wcat[...] = jnp.concatenate([wv[...], wq[...]], axis=1)
    norm_gain = ng_ref[...].reshape(1, width)
    for i in range(steps):
        tok_loads[i].wait()
        cols = slice(i * step_rows, (i + 1) * step_rows)
        x = tok[cols, :].astype(F32)
        row_scale = lax.rsqrt(jnp.mean(x * x, axis=1, keepdims=True) + 1e-06)
        scaled = (x * norm_gain).astype(BF16)
        vq = dot(scaled, wcat[...], ((1,), (0,))) * row_scale
        k = dot(scaled, wk[...], ((1,), (0,))) * row_scale
        vq = vq.T
        for h in range(HEADS):
            vt[h, 0:VDIM, cols] = vq[h * VDIM : (h + 1) * VDIM, :].astype(BF16)
        qt[:, cols] = vq[HEADS * VDIM :, :]
        knat[cols, :] = k.astype(BF16)
        kt[:, cols] = k.T

    masked = in_last.astype(BF16)
    for h in range(HEADS):
        write_features(fk, h, kt[h * FEAT : (h + 1) * FEAT, :], (1.0, 1.0, 1.0, 1.0), None)
        state = dot(fk[h], vt[h] * masked, ((1,), (1,)))
        part = PLANE // HEADS
        st[h * part : (h + 1) * part] = state.astype(BF16).reshape(part, CHUNK, VROWS)

    pl.semaphore_wait(barrier, len(partners))

    sends = []

    def send(src, dst, ssem, rsem, who):
        copy = pltpu.make_async_remote_copy(
            src_ref=src, dst_ref=dst, send_sem=ssem, recv_sem=rsem,
            device_id=who, device_id_type=MESH,
        )
        copy.start()
        sends.append(copy)

    def arrived(src, dst, ssem, rsem):
        pltpu.make_async_remote_copy(
            src_ref=src, dst_ref=dst, send_sem=ssem, recv_sem=rsem,
            device_id=(seq, along_mp(1)), device_id_type=MESH,
        ).wait_recv()

    for r in range(1, PLANE):
        to = in_plane(r)
        send(st.at[to], c1.at[p], s1.at[r - 1], r1.at[r - 1], (z * PLANE + to, mp))
    c1[p] = st[p]

    for h in range(HEADS):
        u = qt[h * FEAT : (h + 1) * FEAT, :]
        write_features(fq, h, u, (1 / 16, 1 / 8, 1 / 2, 2.0), from_before)
        q4 = (u * 0.25).astype(BF16)
        zero = jnp.zeros_like(q4)
        qs[h] = jnp.concatenate([q4, zero] if h == 0 else [zero, q4], axis=0)

    for r in range(1, PLANE):
        arrived(st.at[0], c1.at[in_plane(PLANE - r)], s1.at[r - 1], r1.at[r - 1])
    run = jnp.zeros((CHUNK, VROWS), F32)
    for i in range(PLANE):
        run = run * keep_p[i] + c1[i].astype(F32)
    ts[...] = run.astype(BF16)

    for r in range(1, PLANES):
        to = along_z(r)
        send(ts, c2.at[z], s2.at[r - 1], r2.at[r - 1], (to * PLANE + p, mp))
    c2[z] = ts[...]

    def local_terms(h, half):
        t0, s_rows = half * half_rows, (half + 1) * half_rows
        t = slice(t0, t0 + half_rows)
        y = dot(knat[0:s_rows, :], qs[h, :, t], ((1,), (0,))) + 1.0
        s_index = lax.broadcasted_iota(I32, y.shape, 0)
        t_index = lax.broadcasted_iota(I32, (1, half_rows), 1) + t0
        seen = (s_index <= t_index) & (s_index >= low_row[:, t])
        weight = jnp.where(seen, y * y + 1.0, 0.0).astype(BF16)
        num[h, :, t] = dot(vt[h, :, 0:s_rows], weight, ((1,), (0,)))

    local_terms(0, 0)
    local_terms(0, 1)

    for r in range(1, PLANES):
        arrived(ts, c2.at[along_z(PLANES - r)], s2.at[r - 1], r2.at[r - 1])
    run = jnp.zeros((CHUNK, VROWS), F32)
    for i in range(PLANES):
        before = i < z
        run = run * jnp.where(before, keep_z[i], 1.0) + c2[i].astype(F32) * jnp.where(
            before, 1.0, 0.0
        )
    for i in range(PLANE):
        rs[i] = run.astype(BF16)
        if i < PLANE - 1:
            run = run * keep_p[i] + c1[i].astype(F32)

    for r in range(1, PLANE):
        to = in_plane(r)
        send(rs.at[to], sin.at[p], s3.at[r - 1], r3.at[r - 1], (z * PLANE + to, mp))
    sin[p] = rs[p]

    local_terms(1, 0)
    local_terms(1, 1)
    ow_load.wait()
    turned = ow[...].T
    ot[...] = turned.reshape(RING, HEADS * VDIM, HEADS * VDIM)

    for r in range(1, PLANE):
        arrived(rs.at[0], sin.at[in_plane(PLANE - r)], s3.at[r - 1], r3.at[r - 1])

    for half in range(2):
        t = slice(half * half_rows, (half + 1) * half_rows)
        for h in range(HEADS):
            part = PLANE // HEADS
            incoming = sin[h * part : (h + 1) * part].reshape(TERMS, VROWS)
            both = num[h, :, t] + dot(incoming, fq[h, :, t], ((0,), (0,)))
            attended = both[0:VDIM, :] * (1.0 / both[VDIM : VDIM + 1, :])
            c = slice(h * VDIM, (h + 1) * VDIM)
            gain = jnp.concatenate([gcol[c, :]] * (half_rows // 128), axis=1)
            ht[half, c, :] = (attended * gain).astype(BF16)

    def share(hops, half):
        return dot(ot[along_mp(hops)], ht[half], ((1,), (0,)))

    def ring(order, i, sign, sbuf, rbuf, ssem, rsem):
        hops, half = order[i]
        block = share(sign * hops, half)
        if (hops + 1, half) in order:
            j = order.index((hops + 1, half))
            arrived(sbuf.at[j], rbuf.at[j], ssem.at[j], rsem.at[j])
            block = block + rbuf[j].astype(F32)
        sbuf[i] = block.astype(BF16)
        send(sbuf.at[i], rbuf.at[i], ssem.at[i], rsem.at[i], (seq, along_mp(sign)))

    for i in range(len(RIGHTWARD)):
        ring(RIGHTWARD, i, 1, send_r, recv_r, ssr, rsr)
        ring(LEFTWARD, i, -1, send_l, recv_l, ssl, rsl)
    own = [share(0, half) for half in range(2)]
    for half in range(2):
        i, j = RIGHTWARD.index((1, half)), LEFTWARD.index((1, half))
        arrived(send_r.at[i], recv_r.at[i], ssr.at[i], rsr.at[i])
        arrived(send_l.at[j], recv_l.at[j], ssl.at[j], rsl.at[j])
        summed = own[half] + recv_r[i].astype(F32) + recv_l[j].astype(F32)
        out_ref[half * half_rows : (half + 1) * half_rows, :] = summed.T.astype(BF16)

    for copy in sends:
        copy.wait_send()


def local(tokens, norm_gain, q_weight, k_weight, v_weight, out_gain, o_weight, lengths):
    rows, width = tokens.shape
    wide = HEADS * VDIM
    half = (wide, rows // 2)
    dma, vmem = pltpu.SemaphoreType.DMA, pltpu.VMEM
    hbm = pl.BlockSpec(memory_space=pl.ANY)
    whole = pl.BlockSpec(memory_space=pltpu.VMEM)
    return pl.pallas_call(
        kernel,
        out_shape=jax.ShapeDtypeStruct((rows, wide), BF16),
        in_specs=[hbm, whole, hbm, hbm, hbm, whole, hbm, pl.BlockSpec(memory_space=pltpu.SMEM)],
        out_specs=whole,
        scratch_shapes=[
            vmem((rows, width), BF16),
            vmem(q_weight.shape, BF16),
            vmem(k_weight.shape, BF16),
            vmem(v_weight.shape, BF16),
            vmem(o_weight.shape, BF16),
            vmem((width, wide + HEADS * FEAT), BF16),
            vmem((RING, wide, wide), BF16),
            vmem((wide, 128), F32),
            vmem((HEADS, VROWS, rows), BF16),
            vmem((HEADS * FEAT, rows), F32),
            vmem((HEADS * FEAT, rows), F32),
            vmem((rows, HEADS * FEAT), BF16),
            vmem((HEADS, HEADS * FEAT, rows), BF16),
            vmem((HEADS, TERMS, rows), BF16),
            vmem((HEADS, TERMS, rows), BF16),
            vmem((HEADS, VROWS, rows), F32),
            vmem((2,) + half, BF16),
            vmem((PLANE, CHUNK, VROWS), BF16),
            vmem((PLANE, CHUNK, VROWS), BF16),
            vmem((CHUNK, VROWS), BF16),
            vmem((PLANES, CHUNK, VROWS), BF16),
            vmem((PLANE, CHUNK, VROWS), BF16),
            vmem((PLANE, CHUNK, VROWS), BF16),
            vmem((len(RIGHTWARD),) + half, BF16),
            vmem((len(LEFTWARD),) + half, BF16),
            vmem((len(RIGHTWARD),) + half, BF16),
            vmem((len(LEFTWARD),) + half, BF16),
            dma((8,)),
            dma((PLANE - 1,)),
            dma((PLANE - 1,)),
            dma((PLANES - 1,)),
            dma((PLANES - 1,)),
            dma((PLANE - 1,)),
            dma((PLANE - 1,)),
            dma((len(RIGHTWARD),)),
            dma((len(RIGHTWARD),)),
            dma((len(LEFTWARD),)),
            dma((len(LEFTWARD),)),
        ],
        compiler_params=pltpu.CompilerParams(
            collective_id=0, has_side_effects=True, vmem_limit_bytes=50 << 20
        ),
    )(tokens, norm_gain, q_weight, k_weight, v_weight, out_gain, o_weight, lengths)


def solution(mesh):
    placed = (
        P("seq", None),
        P(),
        P(None, "mp"),
        P(None, "mp"),
        P(None, "mp"),
        P("mp"),
        P("mp", None),
        P(),
    )
    return jax.shard_map(
        local, mesh=mesh, in_specs=placed, out_specs=P("seq", "mp"), check_vma=False
    )
```

```python
import functools

import jax
import jax.numpy as jnp
from jax import lax
from jax.experimental import pallas as pl
from jax.experimental.pallas import tpu as pltpu
from jax.sharding import PartitionSpec as P

MESH = pl.DeviceIdType.MESH
F32, BF16, I32 = jnp.float32, jnp.bfloat16, jnp.int32

FEAT = 16
VDIM = 112
HEADS = 2
PLANE = 8
PLANES = 8
RING = 8
TERMS = 192
CHUNK = HEADS * TERMS // PLANE
VROWS = 128

RIGHTWARD = ((4, 0), (3, 1), (3, 0), (2, 1), (2, 0), (1, 1), (1, 0))
LEFTWARD = tuple((hops, 1 - half) for hops, half in RIGHTWARD)


def dot(a, b, dims):
    return lax.dot_general(a, b, (dims, ((), ())), preferred_element_type=F32)


def write_features(out, head, u, coefficients, keep):
    square, cross, linear, constant = coefficients
    for d in range(FEAT // 2 + 1):
        turned = u if d == 0 else pltpu.roll(u, d, 0)
        scale = square if d in (0, FEAT // 2) else cross
        rows = u * turned
        if scale != 1.0:
            rows = rows * scale
        if keep is not None:
            rows = rows * keep
        out[head, d * FEAT : (d + 1) * FEAT, :] = rows.astype(BF16)
    base = (FEAT // 2 + 1) * FEAT
    rows = u * linear if linear != 1.0 else u
    if keep is not None:
        rows = rows * keep
    out[head, base : base + FEAT, :] = rows.astype(BF16)
    index = lax.broadcasted_iota(I32, (2 * FEAT, u.shape[1]), 0)
    rows = jnp.where(index == 0, constant, 0.0)
    if keep is not None:
        rows = rows * keep
    out[head, base + FEAT : base + 3 * FEAT, :] = rows.astype(BF16)


def kernel(
    tok_hbm, ng_hbm, wq_hbm, wk_hbm, wv_hbm, og_hbm, ow_hbm, len_hbm,
    out_ref,
    len_ref, ng_ref, og_ref, tok, weights, ow, ot, gcol,
    vt, qt, kt, knat, qs, fk, fq, num, ht,
    st, c1, ts, c2, rs, sin, send_r, send_l, recv_r, recv_l,
    load_sem, s1, r1, s2, r2, s3, r3, ssr, rsr, ssl, rsl,
):
    rows, width = tok.shape
    half_rows = rows // 2
    seq, mp = lax.axis_index("seq"), lax.axis_index("mp")
    z, p = lax.div(seq, PLANE), lax.rem(seq, PLANE)
    first_row = seq * rows

    def in_plane(r):
        return lax.rem(p + r, PLANE)

    def along_z(r):
        return lax.rem(z + r, PLANES)

    def along_mp(r):
        return lax.rem(mp + r + RING, RING)

    barrier = pltpu.get_barrier_semaphore()
    partners = [(z * PLANE + in_plane(r), mp) for r in range(1, PLANE)]
    partners += [(along_z(r) * PLANE + p, mp) for r in range(1, PLANES)]
    partners += [(seq, along_mp(1)), (seq, along_mp(-1))]
    for who in partners:
        pl.semaphore_signal(barrier, inc=1, device_id=who, device_id_type=MESH)

    steps = 2
    step_rows = rows // steps
    len_load = pltpu.make_async_copy(len_hbm, len_ref, load_sem.at[6])
    ng_load = pltpu.make_async_copy(ng_hbm, ng_ref, load_sem.at[7])
    og_load = pltpu.make_async_copy(og_hbm, og_ref, load_sem.at[8])
    loads, base = [], 0
    for i, src in enumerate((wv_hbm, wq_hbm, wk_hbm)):
        dst = weights.at[pl.ds(base, src.shape[0]), :]
        loads.append(pltpu.make_async_copy(src, dst, load_sem.at[i]))
        base += src.shape[0]
    tok_loads = [
        pltpu.make_async_copy(
            tok_hbm.at[pl.ds(i * step_rows, step_rows), :],
            tok.at[pl.ds(i * step_rows, step_rows), :],
            load_sem.at[4 + i],
        )
        for i in range(steps)
    ]
    ow_load = pltpu.make_async_copy(ow_hbm, ow, load_sem.at[3])
    for c in [len_load, ng_load] + loads + tok_loads + [og_load, ow_load]:
        c.start()
    len_load.wait()

    lens = [len_ref[i] for i in range(len_ref.shape[0])]
    ends, total = [], None
    for n in lens:
        total = n if total is None else total + n
        ends.append(total)

    def start_of(position):
        found = 0
        for n, e in zip(lens, ends):
            found = found + jnp.where(e <= position, n, 0)
        return found

    pos_row = first_row + lax.broadcasted_iota(I32, (1, rows), 1)
    starts_row = start_of(pos_row)
    low_row = starts_row - first_row
    last_start = start_of(first_row + rows - 1)
    in_last = jnp.where(pos_row >= last_start, 1.0, 0.0).astype(F32)
    from_before = jnp.where(starts_row < first_row, 1.0, 0.0).astype(F32)

    def kept(row0, count):
        goes_on = start_of(row0 + count - 1) < row0
        return jnp.where(goes_on, 1.0, 0.0).astype(F32)

    plane_rows = PLANE * rows
    keep_p = [kept(z * plane_rows + i * rows, rows) for i in range(PLANE)]
    keep_z = [kept(i * plane_rows, plane_rows) for i in range(PLANES)]

    index = lax.broadcasted_iota(I32, (VROWS - VDIM, rows), 0)
    ones = jnp.where(index == 0, 1.0, 0.0).astype(BF16)
    for h in range(HEADS):
        vt[h, VDIM:VROWS, :] = ones
    og_load.wait()
    gain_row = og_ref[...].reshape(1, HEADS * VDIM)
    gcol[...] = jnp.broadcast_to(gain_row, (128, HEADS * VDIM)).T

    for c in loads:
        c.wait()
    ng_load.wait()
    norm_gain = ng_ref[...].reshape(1, width)
    for i in range(steps):
        tok_loads[i].wait()
        cols = slice(i * step_rows, (i + 1) * step_rows)
        x = tok[cols, :].astype(F32)
        scaled = (x * norm_gain).astype(BF16)
        squares = x * x
        sums = sum(squares[:, j : j + 128] for j in range(0, width, 128))
        row_scale = lax.rsqrt(jnp.sum(sums.T, axis=0, keepdims=True) / width + 1e-06)
        vqk = dot(weights[...], scaled, ((1,), (1,))) * row_scale
        for h in range(HEADS):
            vt[h, 0:VDIM, cols] = vqk[h * VDIM : (h + 1) * VDIM, :].astype(BF16)
        base = HEADS * VDIM
        qt[:, cols] = vqk[base : base + HEADS * FEAT, :]
        k = vqk[base + HEADS * FEAT :, :]
        kt[:, cols] = k
        knat[cols, :] = k.T.astype(BF16)

    masked = in_last.astype(BF16)
    for h in range(HEADS):
        write_features(fk, h, kt[h * FEAT : (h + 1) * FEAT, :], (1.0, 1.0, 1.0, 1.0), None)
        state = dot(fk[h], vt[h] * masked, ((1,), (1,)))
        part = PLANE // HEADS
        st[h * part : (h + 1) * part] = state.astype(BF16).reshape(part, CHUNK, VROWS)

    pl.semaphore_wait(barrier, len(partners))

    sends = []

    def send(src, dst, ssem, rsem, who):
        copy = pltpu.make_async_remote_copy(
            src_ref=src, dst_ref=dst, send_sem=ssem, recv_sem=rsem,
            device_id=who, device_id_type=MESH,
        )
        copy.start()
        sends.append(copy)

    def arrived(src, dst, ssem, rsem):
        pltpu.make_async_remote_copy(
            src_ref=src, dst_ref=dst, send_sem=ssem, recv_sem=rsem,
            device_id=(seq, along_mp(1)), device_id_type=MESH,
        ).wait_recv()

    for r in range(1, PLANE):
        to = in_plane(r)
        send(st.at[to], c1.at[p], s1.at[r - 1], r1.at[r - 1], (z * PLANE + to, mp))
    c1[p] = st[p]

    for h in range(HEADS):
        u = qt[h * FEAT : (h + 1) * FEAT, :]
        write_features(fq, h, u, (1 / 16, 1 / 8, 1 / 2, 2.0), from_before)
        q4 = (u * 0.25).astype(BF16)
        zero = jnp.zeros_like(q4)
        qs[h] = jnp.concatenate([q4, zero] if h == 0 else [zero, q4], axis=0)

    for r in range(1, PLANE):
        arrived(st.at[0], c1.at[in_plane(PLANE - r)], s1.at[r - 1], r1.at[r - 1])
    run = jnp.zeros((CHUNK, VROWS), F32)
    for i in range(PLANE):
        run = run * keep_p[i] + c1[i].astype(F32)
    ts[...] = run.astype(BF16)

    for r in range(1, PLANES):
        to = along_z(r)
        send(ts, c2.at[z], s2.at[r - 1], r2.at[r - 1], (to * PLANE + p, mp))
    c2[z] = ts[...]

    def local_terms(h, half):
        t0, s_rows = half * half_rows, (half + 1) * half_rows
        t = slice(t0, t0 + half_rows)
        y = dot(knat[0:s_rows, :], qs[h, :, t], ((1,), (0,))) + 1.0
        s_index = lax.broadcasted_iota(I32, y.shape, 0)
        t_index = lax.broadcasted_iota(I32, (1, half_rows), 1) + t0
        seen = (s_index <= t_index) & (s_index >= low_row[:, t])
        weight = jnp.where(seen, y * y + 1.0, 0.0).astype(BF16)
        num[h, :, t] = dot(vt[h, :, 0:s_rows], weight, ((1,), (0,)))

    local_terms(0, 0)
    local_terms(0, 1)

    for r in range(1, PLANES):
        arrived(ts, c2.at[along_z(PLANES - r)], s2.at[r - 1], r2.at[r - 1])
    run = jnp.zeros((CHUNK, VROWS), F32)
    for i in range(PLANES):
        before = i < z
        run = run * jnp.where(before, keep_z[i], 1.0) + c2[i].astype(F32) * jnp.where(
            before, 1.0, 0.0
        )
    for i in range(PLANE):
        rs[i] = run.astype(BF16)
        if i < PLANE - 1:
            run = run * keep_p[i] + c1[i].astype(F32)

    for r in range(1, PLANE):
        to = in_plane(r)
        send(rs.at[to], sin.at[p], s3.at[r - 1], r3.at[r - 1], (z * PLANE + to, mp))
    sin[p] = rs[p]

    local_terms(1, 0)
    local_terms(1, 1)
    ow_load.wait()
    turned = ow[...].T
    ot[...] = turned.reshape(RING, HEADS * VDIM, HEADS * VDIM)

    for r in range(1, PLANE):
        arrived(rs.at[0], sin.at[in_plane(PLANE - r)], s3.at[r - 1], r3.at[r - 1])

    for half in range(2):
        t = slice(half * half_rows, (half + 1) * half_rows)
        for h in range(HEADS):
            part = PLANE // HEADS
            incoming = sin[h * part : (h + 1) * part].reshape(TERMS, VROWS)
            both = num[h, :, t] + dot(incoming, fq[h, :, t], ((0,), (0,)))
            attended = both[0:VDIM, :] * (1.0 / both[VDIM : VDIM + 1, :])
            c = slice(h * VDIM, (h + 1) * VDIM)
            gain = jnp.concatenate([gcol[c, :]] * (half_rows // 128), axis=1)
            ht[half, c, :] = (attended * gain).astype(BF16)

    def share(hops, half):
        return dot(ot[along_mp(hops)], ht[half], ((1,), (0,)))

    def ring(order, i, sign, sbuf, rbuf, ssem, rsem):
        hops, half = order[i]
        block = share(sign * hops, half)
        if (hops + 1, half) in order:
            j = order.index((hops + 1, half))
            arrived(sbuf.at[j], rbuf.at[j], ssem.at[j], rsem.at[j])
            block = block + rbuf[j].astype(F32)
        sbuf[i] = block.astype(BF16)
        send(sbuf.at[i], rbuf.at[i], ssem.at[i], rsem.at[i], (seq, along_mp(sign)))

    for i in range(len(RIGHTWARD)):
        ring(RIGHTWARD, i, 1, send_r, recv_r, ssr, rsr)
        ring(LEFTWARD, i, -1, send_l, recv_l, ssl, rsl)
    own = [share(0, half) for half in range(2)]
    for half in range(2):
        i, j = RIGHTWARD.index((1, half)), LEFTWARD.index((1, half))
        arrived(send_r.at[i], recv_r.at[i], ssr.at[i], rsr.at[i])
        arrived(send_l.at[j], recv_l.at[j], ssl.at[j], rsl.at[j])
        summed = own[half] + recv_r[i].astype(F32) + recv_l[j].astype(F32)
        out_ref[:, half * half_rows : (half + 1) * half_rows] = summed.astype(BF16)

    for copy in sends:
        copy.wait_send()


def local(tokens, norm_gain, q_weight, k_weight, v_weight, out_gain, o_weight, lengths):
    rows, width = tokens.shape
    wide = HEADS * VDIM
    half = (wide, rows // 2)
    dma, vmem = pltpu.SemaphoreType.DMA, pltpu.VMEM
    hbm = pl.BlockSpec(memory_space=pltpu.HBM)
    whole = pl.BlockSpec(memory_space=pltpu.VMEM)
    turned = pl.pallas_call(
        kernel,
        out_shape=jax.ShapeDtypeStruct((wide, rows), BF16),
        in_specs=[hbm] * 8,
        out_specs=whole,
        scratch_shapes=[
            pltpu.SMEM(lengths.shape, I32),
            vmem(norm_gain.shape, F32),
            vmem(out_gain.shape, F32),
            vmem((rows, width), BF16),
            vmem((wide + 2 * HEADS * FEAT, width), BF16),
            vmem(o_weight.shape, BF16),
            vmem((RING, wide, wide), BF16),
            vmem((wide, 128), F32),
            vmem((HEADS, VROWS, rows), BF16),
            vmem((HEADS * FEAT, rows), F32),
            vmem((HEADS * FEAT, rows), F32),
            vmem((rows, HEADS * FEAT), BF16),
            vmem((HEADS, HEADS * FEAT, rows), BF16),
            vmem((HEADS, TERMS, rows), BF16),
            vmem((HEADS, TERMS, rows), BF16),
            vmem((HEADS, VROWS, rows), F32),
            vmem((2,) + half, BF16),
            vmem((PLANE, CHUNK, VROWS), BF16),
            vmem((PLANE, CHUNK, VROWS), BF16),
            vmem((CHUNK, VROWS), BF16),
            vmem((PLANES, CHUNK, VROWS), BF16),
            vmem((PLANE, CHUNK, VROWS), BF16),
            vmem((PLANE, CHUNK, VROWS), BF16),
            vmem((len(RIGHTWARD),) + half, BF16),
            vmem((len(LEFTWARD),) + half, BF16),
            vmem((len(RIGHTWARD),) + half, BF16),
            vmem((len(LEFTWARD),) + half, BF16),
            dma((9,)),
            dma((PLANE - 1,)),
            dma((PLANE - 1,)),
            dma((PLANES - 1,)),
            dma((PLANES - 1,)),
            dma((PLANE - 1,)),
            dma((PLANE - 1,)),
            dma((len(RIGHTWARD),)),
            dma((len(RIGHTWARD),)),
            dma((len(LEFTWARD),)),
            dma((len(LEFTWARD),)),
        ],
        compiler_params=pltpu.CompilerParams(
            collective_id=0, has_side_effects=True, vmem_limit_bytes=58 << 20
        ),
    )(tokens, norm_gain, q_weight.T, k_weight.T, v_weight.T, out_gain, o_weight, lengths)
    return turned.T


def solution(mesh):
    placed = (
        P("seq", None),
        P(),
        P(None, "mp"),
        P(None, "mp"),
        P(None, "mp"),
        P("mp"),
        P("mp", None),
        P(),
    )
    return jax.shard_map(
        local, mesh=mesh, in_specs=placed, out_specs=P("seq", "mp"), check_vma=False
    )
```

```python
import functools

import jax
import jax.numpy as jnp
from jax import lax
from jax.experimental import pallas as pl
from jax.experimental.pallas import tpu as pltpu
from jax.sharding import PartitionSpec as P

MESH = pl.DeviceIdType.MESH
F32, BF16, I32 = jnp.float32, jnp.bfloat16, jnp.int32

FEAT = 16
VDIM = 112
HEADS = 2
PLANE = 8
PLANES = 8
RING = 8
TERMS = 192
CHUNK = HEADS * TERMS // PLANE
VROWS = 128

RIGHTWARD = ((4, 0), (3, 1), (3, 0), (2, 1), (2, 0), (1, 1), (1, 0))
LEFTWARD = tuple((hops, 1 - half) for hops, half in RIGHTWARD)


def dot(a, b, dims):
    return lax.dot_general(a, b, (dims, ((), ())), preferred_element_type=F32)


def write_features(out, head, u, coefficients, keep):
    square, cross, linear, constant = coefficients
    for d in range(FEAT // 2 + 1):
        turned = u if d == 0 else pltpu.roll(u, d, 0)
        scale = square if d in (0, FEAT // 2) else cross
        rows = u * turned
        if scale != 1.0:
            rows = rows * scale
        if keep is not None:
            rows = rows * keep
        out[head, d * FEAT : (d + 1) * FEAT, :] = rows.astype(BF16)
    base = (FEAT // 2 + 1) * FEAT
    rows = u * linear if linear != 1.0 else u
    if keep is not None:
        rows = rows * keep
    out[head, base : base + FEAT, :] = rows.astype(BF16)
    index = lax.broadcasted_iota(I32, (2 * FEAT, u.shape[1]), 0)
    rows = jnp.where(index == 0, constant, 0.0)
    if keep is not None:
        rows = rows * keep
    out[head, base + FEAT : base + 3 * FEAT, :] = rows.astype(BF16)


def kernel(
    tok_hbm, ng_hbm, wq_hbm, wk_hbm, wv_hbm, og_hbm, ow_hbm, len_hbm,
    out_ref,
    len_ref, ng_ref, og_ref, tok, weights, ow, ot, gcol,
    vt, qt, kt, knat, qs, fk, fq, num, ht,
    st, c1, ts, c2, rs, sin, send_r, send_l, recv_r, recv_l,
    load_sem, s1, r1, s2, r2, s3, r3, ssr, rsr, ssl, rsl, near_sem, far_sem,
):
    rows, width = tok.shape
    half_rows = rows // 2
    seq, mp = lax.axis_index("seq"), lax.axis_index("mp")
    z, p = lax.div(seq, PLANE), lax.rem(seq, PLANE)
    first_row = seq * rows

    def in_plane(r):
        return lax.rem(p + r, PLANE)

    def along_z(r):
        return lax.rem(z + r, PLANES)

    def along_mp(r):
        return lax.rem(mp + r + RING, RING)

    def in_line(r):
        return ((z + r) * PLANE + p, mp)

    def on_later_planes(act, steps=range(1, PLANES)):
        for r in steps:
            pl.when(z + r < PLANES)(functools.partial(act, r))

    def on_earlier_planes(act):
        for r in range(1, PLANES):
            pl.when(z >= r)(functools.partial(act, r))

    barrier = pltpu.get_barrier_semaphore()
    partners = [(z * PLANE + in_plane(r), mp) for r in range(1, PLANE)]
    partners += [(seq, along_mp(1)), (seq, along_mp(-1))]
    for who in partners:
        pl.semaphore_signal(barrier, inc=1, device_id=who, device_id_type=MESH)
    on_later_planes(
        lambda r: pl.semaphore_signal(barrier, inc=1, device_id=in_line(r), device_id_type=MESH)
    )

    steps = 2
    step_rows = rows // steps
    len_load = pltpu.make_async_copy(len_hbm, len_ref, load_sem.at[6])
    ng_load = pltpu.make_async_copy(ng_hbm, ng_ref, load_sem.at[7])
    og_load = pltpu.make_async_copy(og_hbm, og_ref, load_sem.at[8])
    loads, base = [], 0
    for i, src in enumerate((wv_hbm, wq_hbm, wk_hbm)):
        dst = weights.at[pl.ds(base, src.shape[0]), :]
        loads.append(pltpu.make_async_copy(src, dst, load_sem.at[i]))
        base += src.shape[0]
    tok_loads = [
        pltpu.make_async_copy(
            tok_hbm.at[pl.ds(i * step_rows, step_rows), :],
            tok.at[pl.ds(i * step_rows, step_rows), :],
            load_sem.at[4 + i],
        )
        for i in range(steps)
    ]
    ow_load = pltpu.make_async_copy(ow_hbm, ow, load_sem.at[3])
    for c in [len_load, ng_load] + loads + tok_loads + [og_load, ow_load]:
        c.start()
    len_load.wait()

    lens = [len_ref[i] for i in range(len_ref.shape[0])]
    ends, total = [], None
    for n in lens:
        total = n if total is None else total + n
        ends.append(total)

    def start_of(position):
        found = 0
        for n, e in zip(lens, ends):
            found = found + jnp.where(e <= position, n, 0)
        return found

    pos_row = first_row + lax.broadcasted_iota(I32, (1, rows), 1)
    starts_row = start_of(pos_row)
    low_row = starts_row - first_row
    last_start = start_of(first_row + rows - 1)
    in_last = jnp.where(pos_row >= last_start, 1.0, 0.0).astype(F32)
    from_before = jnp.where(starts_row < first_row, 1.0, 0.0).astype(F32)

    def kept(row0, count):
        goes_on = start_of(row0 + count - 1) < row0
        return jnp.where(goes_on, 1.0, 0.0).astype(F32)

    plane_rows = PLANE * rows
    keep_p = [kept(z * plane_rows + i * rows, rows) for i in range(PLANE)]
    keep_z = [kept(i * plane_rows, plane_rows) for i in range(PLANES)]

    index = lax.broadcasted_iota(I32, (VROWS - VDIM, rows), 0)
    ones = jnp.where(index == 0, 1.0, 0.0).astype(BF16)
    for h in range(HEADS):
        vt[h, VDIM:VROWS, :] = ones
    for i in range(PLANES):

        @pl.when(i >= z)
        def _():
            c2[i] = jnp.zeros((CHUNK, VROWS), BF16)

    og_load.wait()
    gain_row = og_ref[...].reshape(1, HEADS * VDIM)
    gcol[...] = jnp.broadcast_to(gain_row, (128, HEADS * VDIM)).T

    for c in loads:
        c.wait()
    ng_load.wait()
    norm_gain = ng_ref[...].reshape(1, width)
    for i in range(steps):
        tok_loads[i].wait()
        cols = slice(i * step_rows, (i + 1) * step_rows)
        x = tok[cols, :].astype(F32)
        scaled = (x * norm_gain).astype(BF16)
        squares = x * x
        sums = sum(squares[:, j : j + 128] for j in range(0, width, 128))
        row_scale = lax.rsqrt(jnp.sum(sums.T, axis=0, keepdims=True) / width + 1e-06)
        vqk = dot(weights[...], scaled, ((1,), (1,))) * row_scale
        for h in range(HEADS):
            vt[h, 0:VDIM, cols] = vqk[h * VDIM : (h + 1) * VDIM, :].astype(BF16)
        base = HEADS * VDIM
        qt[:, cols] = vqk[base : base + HEADS * FEAT, :]
        k = vqk[base + HEADS * FEAT :, :]
        kt[:, cols] = k
        knat[cols, :] = k.T.astype(BF16)

    masked = in_last.astype(BF16)
    for h in range(HEADS):
        write_features(fk, h, kt[h * FEAT : (h + 1) * FEAT, :], (1.0, 1.0, 1.0, 1.0), None)
        state = dot(fk[h], vt[h] * masked, ((1,), (1,)))
        part = PLANE // HEADS
        st[h * part : (h + 1) * part] = state.astype(BF16).reshape(part, CHUNK, VROWS)

    pl.semaphore_wait(barrier, len(partners) + z)

    far_half = PLANES // 2
    upper = lax.div(z, far_half)

    def say_ready(r):
        same = lax.div(z - r, far_half) == upper

        @pl.when(same)
        def _():
            pl.semaphore_signal(near_sem, inc=1, device_id=in_line(-r), device_id_type=MESH)

        @pl.when(jnp.logical_not(same))
        def _():
            pl.semaphore_signal(far_sem, inc=1, device_id=in_line(-r), device_id_type=MESH)

    on_earlier_planes(say_ready)

    sends = []

    def remote(src, dst, ssem, rsem, who):
        return pltpu.make_async_remote_copy(
            src_ref=src, dst_ref=dst, send_sem=ssem, recv_sem=rsem,
            device_id=who, device_id_type=MESH,
        )

    def send(src, dst, ssem, rsem, who):
        copy = remote(src, dst, ssem, rsem, who)
        copy.start()
        sends.append(copy)

    def arrived(src, dst, ssem, rsem):
        remote(src, dst, ssem, rsem, (seq, along_mp(1))).wait_recv()

    for r in range(1, PLANE):
        to = in_plane(r)
        send(st.at[to], c1.at[p], s1.at[r - 1], r1.at[r - 1], (z * PLANE + to, mp))
    c1[p] = st[p]

    for h in range(HEADS):
        u = qt[h * FEAT : (h + 1) * FEAT, :]
        write_features(fq, h, u, (1 / 16, 1 / 8, 1 / 2, 2.0), from_before)
        q4 = (u * 0.25).astype(BF16)
        zero = jnp.zeros_like(q4)
        qs[h] = jnp.concatenate([q4, zero] if h == 0 else [zero, q4], axis=0)

    for r in range(1, PLANE):
        arrived(st.at[0], c1.at[in_plane(PLANE - r)], s1.at[r - 1], r1.at[r - 1])
    run = jnp.zeros((CHUNK, VROWS), F32)
    for i in range(PLANE):
        run = run * keep_p[i] + c1[i].astype(F32)
    ts[...] = run.astype(BF16)

    def to_later(r):
        return remote(ts, c2.at[z], s2.at[r - 1], r2.at[r - 1], in_line(r))

    def to_near(r):
        @pl.when(lax.div(z + r, far_half) == upper)
        def _():
            to_later(r).start()

    def to_far(r):
        @pl.when(lax.div(z + r, far_half) != upper)
        def _():
            to_later(r).start()

    later_near = far_half - 1 - lax.rem(z, far_half)
    pl.when(later_near > 0)(lambda: pl.semaphore_wait(near_sem, later_near))
    on_later_planes(to_near, range(1, far_half))

    def local_terms(h, half):
        t0, s_rows = half * half_rows, (half + 1) * half_rows
        t = slice(t0, t0 + half_rows)
        y = dot(knat[0:s_rows, :], qs[h, :, t], ((1,), (0,))) + 1.0
        s_index = lax.broadcasted_iota(I32, y.shape, 0)
        t_index = lax.broadcasted_iota(I32, (1, half_rows), 1) + t0
        seen = (s_index <= t_index) & (s_index >= low_row[:, t])
        weight = jnp.where(seen, y * y + 1.0, 0.0).astype(BF16)
        num[h, :, t] = dot(vt[h, :, 0:s_rows], weight, ((1,), (0,)))

    local_terms(0, 0)
    local_terms(0, 1)

    on_earlier_planes(lambda r: arrived(ts, c2.at[z - r], s2.at[r - 1], r2.at[r - 1]))
    run = jnp.zeros((CHUNK, VROWS), F32)
    for i in range(PLANES):
        run = run * jnp.where(i < z, keep_z[i], 1.0) + c2[i].astype(F32)
    for i in range(PLANE):
        rs[i] = run.astype(BF16)
        if i < PLANE - 1:
            run = run * keep_p[i] + c1[i].astype(F32)

    for r in range(1, PLANE):
        to = in_plane(r)
        send(rs.at[to], sin.at[p], s3.at[r - 1], r3.at[r - 1], (z * PLANE + to, mp))
    sin[p] = rs[p]
    pl.when(upper == 0)(lambda: pl.semaphore_wait(far_sem, far_half))
    on_later_planes(to_far)

    local_terms(1, 0)
    local_terms(1, 1)
    ow_load.wait()
    turned = ow[...].T
    ot[...] = turned.reshape(RING, HEADS * VDIM, HEADS * VDIM)

    for r in range(1, PLANE):
        arrived(rs.at[0], sin.at[in_plane(PLANE - r)], s3.at[r - 1], r3.at[r - 1])

    for half in range(2):
        t = slice(half * half_rows, (half + 1) * half_rows)
        for h in range(HEADS):
            part = PLANE // HEADS
            incoming = sin[h * part : (h + 1) * part].reshape(TERMS, VROWS)
            both = num[h, :, t] + dot(incoming, fq[h, :, t], ((0,), (0,)))
            attended = both[0:VDIM, :] * (1.0 / both[VDIM : VDIM + 1, :])
            c = slice(h * VDIM, (h + 1) * VDIM)
            gain = jnp.concatenate([gcol[c, :]] * (half_rows // 128), axis=1)
            ht[half, c, :] = (attended * gain).astype(BF16)

    def share(hops, half):
        return dot(ot[along_mp(hops)], ht[half], ((1,), (0,)))

    def ring(order, i, sign, sbuf, rbuf, ssem, rsem):
        hops, half = order[i]
        block = share(sign * hops, half)
        if (hops + 1, half) in order:
            j = order.index((hops + 1, half))
            arrived(sbuf.at[j], rbuf.at[j], ssem.at[j], rsem.at[j])
            block = block + rbuf[j].astype(F32)
        sbuf[i] = block.astype(BF16)
        send(sbuf.at[i], rbuf.at[i], ssem.at[i], rsem.at[i], (seq, along_mp(sign)))

    for i in range(len(RIGHTWARD)):
        ring(RIGHTWARD, i, 1, send_r, recv_r, ssr, rsr)
        ring(LEFTWARD, i, -1, send_l, recv_l, ssl, rsl)
    own = [share(0, half) for half in range(2)]
    for half in range(2):
        i, j = RIGHTWARD.index((1, half)), LEFTWARD.index((1, half))
        arrived(send_r.at[i], recv_r.at[i], ssr.at[i], rsr.at[i])
        arrived(send_l.at[j], recv_l.at[j], ssl.at[j], rsl.at[j])
        summed = own[half] + recv_r[i].astype(F32) + recv_l[j].astype(F32)
        out_ref[:, half * half_rows : (half + 1) * half_rows] = summed.astype(BF16)

    for copy in sends:
        copy.wait_send()
    on_later_planes(lambda r: to_later(r).wait_send())


def local(tokens, norm_gain, q_weight, k_weight, v_weight, out_gain, o_weight, lengths):
    rows, width = tokens.shape
    wide = HEADS * VDIM
    half = (wide, rows // 2)
    dma, vmem = pltpu.SemaphoreType.DMA, pltpu.VMEM
    hbm = pl.BlockSpec(memory_space=pltpu.HBM)
    whole = pl.BlockSpec(memory_space=pltpu.VMEM)
    turned = pl.pallas_call(
        kernel,
        out_shape=jax.ShapeDtypeStruct((wide, rows), BF16),
        in_specs=[hbm] * 8,
        out_specs=whole,
        scratch_shapes=[
            pltpu.SMEM(lengths.shape, I32),
            vmem(norm_gain.shape, F32),
            vmem(out_gain.shape, F32),
            vmem((rows, width), BF16),
            vmem((wide + 2 * HEADS * FEAT, width), BF16),
            vmem(o_weight.shape, BF16),
            vmem((RING, wide, wide), BF16),
            vmem((wide, 128), F32),
            vmem((HEADS, VROWS, rows), BF16),
            vmem((HEADS * FEAT, rows), F32),
            vmem((HEADS * FEAT, rows), F32),
            vmem((rows, HEADS * FEAT), BF16),
            vmem((HEADS, HEADS * FEAT, rows), BF16),
            vmem((HEADS, TERMS, rows), BF16),
            vmem((HEADS, TERMS, rows), BF16),
            vmem((HEADS, VROWS, rows), F32),
            vmem((2,) + half, BF16),
            vmem((PLANE, CHUNK, VROWS), BF16),
            vmem((PLANE, CHUNK, VROWS), BF16),
            vmem((CHUNK, VROWS), BF16),
            vmem((PLANES, CHUNK, VROWS), BF16),
            vmem((PLANE, CHUNK, VROWS), BF16),
            vmem((PLANE, CHUNK, VROWS), BF16),
            vmem((len(RIGHTWARD),) + half, BF16),
            vmem((len(LEFTWARD),) + half, BF16),
            vmem((len(RIGHTWARD),) + half, BF16),
            vmem((len(LEFTWARD),) + half, BF16),
            dma((9,)),
            dma((PLANE - 1,)),
            dma((PLANE - 1,)),
            dma((PLANES - 1,)),
            dma((PLANES - 1,)),
            dma((PLANE - 1,)),
            dma((PLANE - 1,)),
            dma((len(RIGHTWARD),)),
            dma((len(RIGHTWARD),)),
            dma((len(LEFTWARD),)),
            dma((len(LEFTWARD),)),
            pltpu.SemaphoreType.REGULAR,
            pltpu.SemaphoreType.REGULAR,
        ],
        compiler_params=pltpu.CompilerParams(
            collective_id=0, has_side_effects=True, vmem_limit_bytes=58 << 20
        ),
    )(tokens, norm_gain, q_weight.T, k_weight.T, v_weight.T, out_gain, o_weight, lengths)
    return turned.T


def solution(mesh):
    placed = (
        P("seq", None),
        P(),
        P(None, "mp"),
        P(None, "mp"),
        P(None, "mp"),
        P("mp"),
        P("mp", None),
        P(),
    )
    return jax.shard_map(
        local, mesh=mesh, in_specs=placed, out_specs=P("seq", "mp"), check_vma=False
    )
```

```python
import functools

import jax
import jax.numpy as jnp
from jax import lax
from jax.experimental import pallas as pl
from jax.experimental.pallas import tpu as pltpu
from jax.sharding import PartitionSpec as P

MESH = pl.DeviceIdType.MESH
F32, BF16, I32 = jnp.float32, jnp.bfloat16, jnp.int32

FEAT = 16
VDIM = 112
HEADS = 2
PLANE = 8
PLANES = 8
RING = 8
TERMS = 192
CHUNK = HEADS * TERMS // PLANE
VROWS = 128

QUARTERS = 4
RIGHTWARD = ((4, 0), (4, 1)) + tuple((k, q) for k in (3, 2, 1) for q in (2, 3, 0, 1))
LEFTWARD = tuple((hops, (quarter + 2) % QUARTERS) for hops, quarter in RIGHTWARD)


def dot(a, b, dims):
    return lax.dot_general(a, b, (dims, ((), ())), preferred_element_type=F32)


def write_features(out, head, u, coefficients, keep):
    square, cross, linear, constant = coefficients
    for d in range(FEAT // 2 + 1):
        turned = u if d == 0 else pltpu.roll(u, d, 0)
        scale = square if d in (0, FEAT // 2) else cross
        rows = u * turned
        if scale != 1.0:
            rows = rows * scale
        if keep is not None:
            rows = rows * keep
        out[head, d * FEAT : (d + 1) * FEAT, :] = rows.astype(BF16)
    base = (FEAT // 2 + 1) * FEAT
    rows = u * linear if linear != 1.0 else u
    if keep is not None:
        rows = rows * keep
    out[head, base : base + FEAT, :] = rows.astype(BF16)
    index = lax.broadcasted_iota(I32, (2 * FEAT, u.shape[1]), 0)
    rows = jnp.where(index == 0, constant, 0.0)
    if keep is not None:
        rows = rows * keep
    out[head, base + FEAT : base + 3 * FEAT, :] = rows.astype(BF16)


def kernel(
    tok_hbm, ng_hbm, wq_hbm, wk_hbm, wv_hbm, og_hbm, ow_hbm, len_hbm,
    out_ref,
    len_ref, ng_ref, og_ref, tok, weights, ow, ot, gcol,
    vt, qt, kt, knat, qs, fk, fq, num, ht, own,
    st, c1, ts, c2, rs, sin, send_r, send_l, recv_r, recv_l,
    load_sem, s1, r1, s2, r2, s3, r3, ssr, rsr, ssl, rsl, near_sem, far_sem,
):
    rows, width = tok.shape
    half_rows, quarter_rows = rows // 2, rows // QUARTERS
    seq, mp = lax.axis_index("seq"), lax.axis_index("mp")
    z, p = lax.div(seq, PLANE), lax.rem(seq, PLANE)
    first_row = seq * rows

    def in_plane(r):
        return lax.rem(p + r, PLANE)

    def along_z(r):
        return lax.rem(z + r, PLANES)

    def along_mp(r):
        return lax.rem(mp + r + RING, RING)

    def in_line(r):
        return ((z + r) * PLANE + p, mp)

    def on_later_planes(act, steps=range(1, PLANES)):
        for r in steps:
            pl.when(z + r < PLANES)(functools.partial(act, r))

    def on_earlier_planes(act):
        for r in range(1, PLANES):
            pl.when(z >= r)(functools.partial(act, r))

    steps = 2
    step_rows = rows // steps
    len_load = pltpu.make_async_copy(len_hbm, len_ref, load_sem.at[6])
    ng_load = pltpu.make_async_copy(ng_hbm, ng_ref, load_sem.at[7])
    og_load = pltpu.make_async_copy(og_hbm, og_ref, load_sem.at[8])
    loads, base = [], 0
    for i, src in enumerate((wv_hbm, wq_hbm, wk_hbm)):
        dst = weights.at[pl.ds(base, src.shape[0]), :]
        loads.append(pltpu.make_async_copy(src, dst, load_sem.at[i]))
        base += src.shape[0]
    tok_loads = [
        pltpu.make_async_copy(
            tok_hbm.at[pl.ds(i * step_rows, step_rows), :],
            tok.at[pl.ds(i * step_rows, step_rows), :],
            load_sem.at[4 + i],
        )
        for i in range(steps)
    ]
    ow_load = pltpu.make_async_copy(ow_hbm, ow, load_sem.at[3])
    for c in [len_load, ng_load] + loads + tok_loads + [og_load, ow_load]:
        c.start()

    barrier = pltpu.get_barrier_semaphore()
    partners = [(z * PLANE + in_plane(r), mp) for r in range(1, PLANE)]
    partners += [(seq, along_mp(1)), (seq, along_mp(-1))]
    for who in partners:
        pl.semaphore_signal(barrier, inc=1, device_id=who, device_id_type=MESH)
    on_later_planes(
        lambda r: pl.semaphore_signal(barrier, inc=1, device_id=in_line(r), device_id_type=MESH)
    )

    len_load.wait()
    lens = [len_ref[i] for i in range(len_ref.shape[0])]
    ends, total = [], None
    for n in lens:
        total = n if total is None else total + n
        ends.append(total)

    def start_of(position):
        found = 0
        for n, e in zip(lens, ends):
            found = found + jnp.where(e <= position, n, 0)
        return found

    pos_row = first_row + lax.broadcasted_iota(I32, (1, rows), 1)
    starts_row = start_of(pos_row)
    low_row = starts_row - first_row
    last_start = start_of(first_row + rows - 1)
    in_last = jnp.where(pos_row >= last_start, 1.0, 0.0).astype(F32)
    from_before = jnp.where(starts_row < first_row, 1.0, 0.0).astype(F32)

    def kept(row0, count):
        goes_on = start_of(row0 + count - 1) < row0
        return jnp.where(goes_on, 1.0, 0.0).astype(F32)

    plane_rows = PLANE * rows
    keep_p = [kept(z * plane_rows + i * rows, rows) for i in range(PLANE)]
    keep_z = [kept(i * plane_rows, plane_rows) for i in range(PLANES)]

    index = lax.broadcasted_iota(I32, (VROWS - VDIM, rows), 0)
    ones = jnp.where(index == 0, 1.0, 0.0).astype(BF16)
    for h in range(HEADS):
        vt[h, VDIM:VROWS, :] = ones
    for i in range(PLANES):

        @pl.when(i >= z)
        def _():
            c2[i] = jnp.zeros((CHUNK, VROWS), BF16)

    og_load.wait()
    gain_row = og_ref[...].reshape(1, HEADS * VDIM)
    gcol[...] = jnp.broadcast_to(gain_row, (128, HEADS * VDIM)).T

    pl.semaphore_wait(barrier, len(partners) + z)

    far_half = PLANES // 2
    upper = lax.div(z, far_half)

    def say_ready(r):
        same = lax.div(z - r, far_half) == upper

        @pl.when(same)
        def _():
            pl.semaphore_signal(near_sem, inc=1, device_id=in_line(-r), device_id_type=MESH)

        @pl.when(jnp.logical_not(same))
        def _():
            pl.semaphore_signal(far_sem, inc=1, device_id=in_line(-r), device_id_type=MESH)

    on_earlier_planes(say_ready)


    for c in loads:
        c.wait()
    ng_load.wait()
    norm_gain = ng_ref[...].reshape(1, width)
    for i in range(steps):
        tok_loads[i].wait()
        cols = slice(i * step_rows, (i + 1) * step_rows)
        x = tok[cols, :].astype(F32)
        scaled = (x * norm_gain).astype(BF16)
        squares = x * x
        sums = sum(squares[:, j : j + 128] for j in range(0, width, 128))
        row_scale = lax.rsqrt(jnp.sum(sums.T, axis=0, keepdims=True) / width + 1e-06)
        vqk = dot(weights[...], scaled, ((1,), (1,))) * row_scale
        for h in range(HEADS):
            vt[h, 0:VDIM, cols] = vqk[h * VDIM : (h + 1) * VDIM, :].astype(BF16)
        base = HEADS * VDIM
        qt[:, cols] = vqk[base : base + HEADS * FEAT, :]
        k = vqk[base + HEADS * FEAT :, :]
        kt[:, cols] = k
        knat[cols, :] = k.T.astype(BF16)

    masked = in_last.astype(BF16)
    for h in range(HEADS):
        write_features(fk, h, kt[h * FEAT : (h + 1) * FEAT, :], (1.0, 1.0, 1.0, 1.0), None)
        state = dot(fk[h], vt[h] * masked, ((1,), (1,)))
        part = PLANE // HEADS
        st[h * part : (h + 1) * part] = state.astype(BF16).reshape(part, CHUNK, VROWS)

    sends = []

    def remote(src, dst, ssem, rsem, who):
        return pltpu.make_async_remote_copy(
            src_ref=src, dst_ref=dst, send_sem=ssem, recv_sem=rsem,
            device_id=who, device_id_type=MESH,
        )

    def send(src, dst, ssem, rsem, who):
        copy = remote(src, dst, ssem, rsem, who)
        copy.start()
        sends.append(copy)

    def arrived(src, dst, ssem, rsem):
        remote(src, dst, ssem, rsem, (seq, along_mp(1))).wait_recv()

    for r in range(1, PLANE):
        to = in_plane(r)
        send(st.at[to], c1.at[p], s1.at[r - 1], r1.at[r - 1], (z * PLANE + to, mp))
    c1[p] = st[p]

    for h in range(HEADS):
        u = qt[h * FEAT : (h + 1) * FEAT, :]
        write_features(fq, h, u, (1 / 16, 1 / 8, 1 / 2, 2.0), from_before)
        q4 = (u * 0.25).astype(BF16)
        zero = jnp.zeros_like(q4)
        qs[h] = jnp.concatenate([q4, zero] if h == 0 else [zero, q4], axis=0)

    for r in range(1, PLANE):
        arrived(st.at[0], c1.at[in_plane(PLANE - r)], s1.at[r - 1], r1.at[r - 1])
    run = jnp.zeros((CHUNK, VROWS), F32)
    for i in range(PLANE):
        run = run * keep_p[i] + c1[i].astype(F32)
    ts[...] = run.astype(BF16)

    def to_later(r):
        return remote(ts, c2.at[z], s2.at[r - 1], r2.at[r - 1], in_line(r))

    def to_near(r):
        @pl.when(lax.div(z + r, far_half) == upper)
        def _():
            to_later(r).start()

    def to_far(r):
        @pl.when(lax.div(z + r, far_half) != upper)
        def _():
            to_later(r).start()

    later_near = far_half - 1 - lax.rem(z, far_half)
    pl.when(later_near > 0)(lambda: pl.semaphore_wait(near_sem, later_near))
    on_later_planes(to_near, range(1, far_half))

    def local_terms(h, half):
        t0, s_rows = half * half_rows, (half + 1) * half_rows
        t = slice(t0, t0 + half_rows)
        y = dot(knat[0:s_rows, :], qs[h, :, t], ((1,), (0,))) + 1.0
        s_index = lax.broadcasted_iota(I32, y.shape, 0)
        t_index = lax.broadcasted_iota(I32, (1, half_rows), 1) + t0
        seen = (s_index <= t_index) & (s_index >= low_row[:, t])
        weight = jnp.where(seen, y * y + 1.0, 0.0).astype(BF16)
        num[h, :, t] = dot(vt[h, :, 0:s_rows], weight, ((1,), (0,)))

    local_terms(0, 0)
    local_terms(0, 1)

    on_earlier_planes(lambda r: arrived(ts, c2.at[z - r], s2.at[r - 1], r2.at[r - 1]))
    run = jnp.zeros((CHUNK, VROWS), F32)
    for i in range(PLANES):
        run = run * jnp.where(i < z, keep_z[i], 1.0) + c2[i].astype(F32)
    for i in range(PLANE):
        rs[i] = run.astype(BF16)
        if i < PLANE - 1:
            run = run * keep_p[i] + c1[i].astype(F32)

    for r in range(1, PLANE):
        to = in_plane(r)
        send(rs.at[to], sin.at[p], s3.at[r - 1], r3.at[r - 1], (z * PLANE + to, mp))
    sin[p] = rs[p]
    pl.when(upper == 0)(lambda: pl.semaphore_wait(far_sem, far_half))
    on_later_planes(to_far)

    local_terms(1, 0)
    local_terms(1, 1)
    ow_load.wait()
    turned = ow[...].T
    ot[...] = turned.reshape(RING, HEADS * VDIM, HEADS * VDIM)

    for r in range(1, PLANE):
        arrived(rs.at[0], sin.at[in_plane(PLANE - r)], s3.at[r - 1], r3.at[r - 1])

    for half in range(2):
        t = slice(half * half_rows, (half + 1) * half_rows)
        for h in range(HEADS):
            part = PLANE // HEADS
            incoming = sin[h * part : (h + 1) * part].reshape(TERMS, VROWS)
            both = num[h, :, t] + dot(incoming, fq[h, :, t], ((0,), (0,)))
            attended = both[0:VDIM, :] * (1.0 / both[VDIM : VDIM + 1, :])
            c = slice(h * VDIM, (h + 1) * VDIM)
            for i in range(2):
                piece = attended[:, i * quarter_rows : (i + 1) * quarter_rows] * gcol[c, :]
                ht[2 * half + i, c, :] = piece.astype(BF16)

    def share(hops, quarter):
        return dot(ot[along_mp(hops)], ht[quarter], ((1,), (0,)))

    def ring(order, i, sign, sbuf, rbuf, ssem, rsem):
        hops, quarter = order[i]
        block = share(sign * hops, quarter)
        if (hops + 1, quarter) in order:
            j = order.index((hops + 1, quarter))
            arrived(sbuf.at[j], rbuf.at[j], ssem.at[j], rsem.at[j])
            block = block + rbuf[j].astype(F32)
        sbuf[i] = block.astype(BF16)
        send(sbuf.at[i], rbuf.at[i], ssem.at[i], rsem.at[i], (seq, along_mp(sign)))

    for i in range(len(RIGHTWARD)):
        ring(RIGHTWARD, i, 1, send_r, recv_r, ssr, rsr)
        ring(LEFTWARD, i, -1, send_l, recv_l, ssl, rsl)
    for quarter in range(QUARTERS):
        own[quarter] = share(0, quarter)
    for quarter in (2, 0, 3, 1):
        i, j = RIGHTWARD.index((1, quarter)), LEFTWARD.index((1, quarter))
        arrived(send_r.at[i], recv_r.at[i], ssr.at[i], rsr.at[i])
        arrived(send_l.at[j], recv_l.at[j], ssl.at[j], rsl.at[j])
        summed = own[quarter] + recv_r[i].astype(F32) + recv_l[j].astype(F32)
        cols = slice(quarter * quarter_rows, (quarter + 1) * quarter_rows)
        out_ref[:, cols] = summed.astype(BF16)

    for copy in sends:
        copy.wait_send()
    on_later_planes(lambda r: to_later(r).wait_send())


def local(tokens, norm_gain, q_weight, k_weight, v_weight, out_gain, o_weight, lengths):
    rows, width = tokens.shape
    wide = HEADS * VDIM
    piece = (wide, rows // QUARTERS)
    dma, vmem = pltpu.SemaphoreType.DMA, pltpu.VMEM
    hbm = pl.BlockSpec(memory_space=pltpu.HBM)
    whole = pl.BlockSpec(memory_space=pltpu.VMEM)
    operands = (
        tokens, norm_gain, q_weight.T, k_weight.T, v_weight.T, out_gain, o_weight, lengths
    )
    turned = pl.pallas_call(
        kernel,
        out_shape=pltpu.VMEM((wide, rows), BF16),
        in_specs=[hbm] * 8,
        out_specs=whole,
        scratch_shapes=[
            pltpu.SMEM(lengths.shape, I32),
            vmem(norm_gain.shape, F32),
            vmem(out_gain.shape, F32),
            vmem((rows, width), BF16),
            vmem((wide + 2 * HEADS * FEAT, width), BF16),
            vmem(o_weight.shape, BF16),
            vmem((RING, wide, wide), BF16),
            vmem((wide, 128), F32),
            vmem((HEADS, VROWS, rows), BF16),
            vmem((HEADS * FEAT, rows), F32),
            vmem((HEADS * FEAT, rows), F32),
            vmem((rows, HEADS * FEAT), BF16),
            vmem((HEADS, HEADS * FEAT, rows), BF16),
            vmem((HEADS, TERMS, rows), BF16),
            vmem((HEADS, TERMS, rows), BF16),
            vmem((HEADS, VROWS, rows), F32),
            vmem((QUARTERS,) + piece, BF16),
            vmem((QUARTERS,) + piece, F32),
            vmem((PLANE, CHUNK, VROWS), BF16),
            vmem((PLANE, CHUNK, VROWS), BF16),
            vmem((CHUNK, VROWS), BF16),
            vmem((PLANES, CHUNK, VROWS), BF16),
            vmem((PLANE, CHUNK, VROWS), BF16),
            vmem((PLANE, CHUNK, VROWS), BF16),
            vmem((len(RIGHTWARD),) + piece, BF16),
            vmem((len(LEFTWARD),) + piece, BF16),
            vmem((len(RIGHTWARD),) + piece, BF16),
            vmem((len(LEFTWARD),) + piece, BF16),
            dma((9,)),
            dma((PLANE - 1,)),
            dma((PLANE - 1,)),
            dma((PLANES - 1,)),
            dma((PLANES - 1,)),
            dma((PLANE - 1,)),
            dma((PLANE - 1,)),
            dma((len(RIGHTWARD),)),
            dma((len(RIGHTWARD),)),
            dma((len(LEFTWARD),)),
            dma((len(LEFTWARD),)),
            pltpu.SemaphoreType.REGULAR,
            pltpu.SemaphoreType.REGULAR,
        ],
        compiler_params=pltpu.CompilerParams(
            collective_id=0, has_side_effects=True, vmem_limit_bytes=40 << 20
        ),
    )(*[pltpu.with_memory_space_constraint(a, pltpu.HBM) for a in operands])
    return turned.T


def solution(mesh):
    placed = (
        P("seq", None),
        P(),
        P(None, "mp"),
        P(None, "mp"),
        P(None, "mp"),
        P("mp"),
        P("mp", None),
        P(),
    )
    return jax.shard_map(
        local, mesh=mesh, in_specs=placed, out_specs=P("seq", "mp"), check_vma=False
    )
```

```python
import functools

import jax
import jax.numpy as jnp
from jax import lax
from jax.experimental import pallas as pl
from jax.experimental.pallas import tpu as pltpu
from jax.sharding import PartitionSpec as P

MESH = pl.DeviceIdType.MESH
F32, BF16, I32 = jnp.float32, jnp.bfloat16, jnp.int32

FEAT = 16
VDIM = 112
HEADS = 2
PLANE = 8
PLANES = 8
RING = 8
TERMS = 192
CHUNK = HEADS * TERMS // PLANE
VROWS = 128

FAR_FIRST = (4, 3, 5, 2, 6, 1, 7)

QUARTERS = 4
RIGHTWARD = ((4, 0), (4, 1)) + tuple((k, q) for k in (3, 2, 1) for q in (2, 3, 0, 1))
LEFTWARD = tuple((hops, (quarter + 2) % QUARTERS) for hops, quarter in RIGHTWARD)


def dot(a, b, dims):
    return lax.dot_general(a, b, (dims, ((), ())), preferred_element_type=F32)


def write_features(out, head, u, coefficients, keep):
    square, cross, linear, constant = coefficients
    for d in range(FEAT // 2 + 1):
        turned = u if d == 0 else pltpu.roll(u, d, 0)
        scale = square if d in (0, FEAT // 2) else cross
        rows = u * turned
        if scale != 1.0:
            rows = rows * scale
        if keep is not None:
            rows = rows * keep
        out[head, d * FEAT : (d + 1) * FEAT, :] = rows.astype(BF16)
    base = (FEAT // 2 + 1) * FEAT
    rows = u * linear if linear != 1.0 else u
    if keep is not None:
        rows = rows * keep
    out[head, base : base + FEAT, :] = rows.astype(BF16)
    index = lax.broadcasted_iota(I32, (2 * FEAT, u.shape[1]), 0)
    rows = jnp.where(index == 0, constant, 0.0)
    if keep is not None:
        rows = rows * keep
    out[head, base + FEAT : base + 3 * FEAT, :] = rows.astype(BF16)


def kernel(
    tok_hbm, ng_hbm, wq_hbm, wk_hbm, wv_hbm, og_hbm, ow_hbm, len_hbm,
    out_ref,
    len_ref, ng_ref, og_ref, tok, weights, ow, ot, gcol,
    vt, qt, kt, knat, qs, fk, fq, num, ht, own,
    st, c1, ts, c2, rs, sin, send_r, send_l, recv_r, recv_l,
    load_sem, s1, r1, s2, r2, s3, r3, ssr, rsr, ssl, rsl, near_sem, far_sem,
):
    rows, width = tok.shape
    half_rows, quarter_rows = rows // 2, rows // QUARTERS
    seq, mp = lax.axis_index("seq"), lax.axis_index("mp")
    z, p = lax.div(seq, PLANE), lax.rem(seq, PLANE)
    first_row = seq * rows

    def in_plane(r):
        return lax.rem(p + r, PLANE)

    def along_z(r):
        return lax.rem(z + r, PLANES)

    def along_mp(r):
        return lax.rem(mp + r + RING, RING)

    def in_line(r):
        return ((z + r) * PLANE + p, mp)

    def on_later_planes(act, steps=range(1, PLANES)):
        for r in steps:
            pl.when(z + r < PLANES)(functools.partial(act, r))

    def on_earlier_planes(act):
        for r in range(1, PLANES):
            pl.when(z >= r)(functools.partial(act, r))

    steps = 1
    step_rows = rows // steps
    len_load = pltpu.make_async_copy(len_hbm, len_ref, load_sem.at[6])
    ng_load = pltpu.make_async_copy(ng_hbm, ng_ref, load_sem.at[7])
    og_load = pltpu.make_async_copy(og_hbm, og_ref, load_sem.at[8])
    loads, base = [], 0
    for i, src in enumerate((wv_hbm, wq_hbm, wk_hbm)):
        dst = weights.at[pl.ds(base, src.shape[0]), :]
        loads.append(pltpu.make_async_copy(src, dst, load_sem.at[i]))
        base += src.shape[0]
    tok_loads = [
        pltpu.make_async_copy(
            tok_hbm.at[pl.ds(i * step_rows, step_rows), :],
            tok.at[pl.ds(i * step_rows, step_rows), :],
            load_sem.at[4 + i],
        )
        for i in range(steps)
    ]
    ow_load = pltpu.make_async_copy(ow_hbm, ow, load_sem.at[3])
    for c in [len_load, ng_load, tok_loads[0]] + loads + [og_load]:
        c.start()

    barrier = pltpu.get_barrier_semaphore()
    partners = [(z * PLANE + in_plane(r), mp) for r in range(1, PLANE)]
    partners += [(seq, along_mp(1)), (seq, along_mp(-1))]
    for who in partners:
        pl.semaphore_signal(barrier, inc=1, device_id=who, device_id_type=MESH)
    on_later_planes(
        lambda r: pl.semaphore_signal(barrier, inc=1, device_id=in_line(r), device_id_type=MESH)
    )

    len_load.wait()
    lens = [len_ref[i] for i in range(len_ref.shape[0])]
    ends, total = [], None
    for n in lens:
        total = n if total is None else total + n
        ends.append(total)

    def start_of(position):
        found = 0
        for n, e in zip(lens, ends):
            found = found + jnp.where(e <= position, n, 0)
        return found

    pos_row = first_row + lax.broadcasted_iota(I32, (1, rows), 1)
    starts_row = start_of(pos_row)
    low_row = starts_row - first_row
    last_start = start_of(first_row + rows - 1)
    in_last = jnp.where(pos_row >= last_start, 1.0, 0.0).astype(F32)
    from_before = jnp.where(starts_row < first_row, 1.0, 0.0).astype(F32)

    def kept(row0, count):
        goes_on = start_of(row0 + count - 1) < row0
        return jnp.where(goes_on, 1.0, 0.0).astype(F32)

    plane_rows = PLANE * rows
    keep_p = [kept(z * plane_rows + i * rows, rows) for i in range(PLANE)]
    keep_z = [kept(i * plane_rows, plane_rows) for i in range(PLANES)]

    index = lax.broadcasted_iota(I32, (VROWS - VDIM, rows), 0)
    ones = jnp.where(index == 0, 1.0, 0.0).astype(BF16)
    for h in range(HEADS):
        vt[h, VDIM:VROWS, :] = ones
    for i in range(PLANES):

        @pl.when(i >= z)
        def _():
            c2[i] = jnp.zeros((CHUNK, VROWS), BF16)

    og_load.wait()
    gain_row = og_ref[...].reshape(1, HEADS * VDIM)
    gcol[...] = jnp.broadcast_to(gain_row, (128, HEADS * VDIM)).T

    pl.semaphore_wait(barrier, len(partners) + z)

    far_half = PLANES // 2
    upper = lax.div(z, far_half)

    def say_ready(r):
        same = lax.div(z - r, far_half) == upper

        @pl.when(same)
        def _():
            pl.semaphore_signal(near_sem, inc=1, device_id=in_line(-r), device_id_type=MESH)

        @pl.when(jnp.logical_not(same))
        def _():
            pl.semaphore_signal(far_sem, inc=1, device_id=in_line(-r), device_id_type=MESH)

    on_earlier_planes(say_ready)


    for c in loads:
        c.wait()
    ng_load.wait()
    norm_gain = ng_ref[...].reshape(1, width)
    for i in range(steps):
        tok_loads[i].wait()
        cols = slice(i * step_rows, (i + 1) * step_rows)
        x = tok[cols, :].astype(F32)
        scaled = (x * norm_gain).astype(BF16)
        squares = x * x
        sums = sum(squares[:, j : j + 128] for j in range(0, width, 128))
        row_scale = lax.rsqrt(jnp.sum(sums.T, axis=0, keepdims=True) / width + 1e-06)
        vqk = dot(weights[...], scaled, ((1,), (1,))) * row_scale
        for h in range(HEADS):
            vt[h, 0:VDIM, cols] = vqk[h * VDIM : (h + 1) * VDIM, :].astype(BF16)
        base = HEADS * VDIM
        qt[:, cols] = vqk[base : base + HEADS * FEAT, :]
        k = vqk[base + HEADS * FEAT :, :]
        kt[:, cols] = k
        knat[cols, :] = k.T.astype(BF16)

    ow_load.start()

    masked = in_last.astype(BF16)
    for h in range(HEADS):
        write_features(fk, h, kt[h * FEAT : (h + 1) * FEAT, :], (1.0, 1.0, 1.0, 1.0), None)
        state = dot(fk[h], vt[h] * masked, ((1,), (1,)))
        part = PLANE // HEADS
        st[h * part : (h + 1) * part] = state.astype(BF16).reshape(part, CHUNK, VROWS)

    sends = []

    def remote(src, dst, ssem, rsem, who):
        return pltpu.make_async_remote_copy(
            src_ref=src, dst_ref=dst, send_sem=ssem, recv_sem=rsem,
            device_id=who, device_id_type=MESH,
        )

    def send(src, dst, ssem, rsem, who):
        copy = remote(src, dst, ssem, rsem, who)
        copy.start()
        sends.append(copy)

    def arrived(src, dst, ssem, rsem):
        remote(src, dst, ssem, rsem, (seq, along_mp(1))).wait_recv()

    for r in FAR_FIRST:
        to = in_plane(r)
        send(st.at[to], c1.at[p], s1.at[r - 1], r1.at[r - 1], (z * PLANE + to, mp))
    c1[p] = st[p]

    for h in range(HEADS):
        u = qt[h * FEAT : (h + 1) * FEAT, :]
        write_features(fq, h, u, (1 / 16, 1 / 8, 1 / 2, 2.0), from_before)
        q4 = (u * 0.25).astype(BF16)
        zero = jnp.zeros_like(q4)
        qs[h] = jnp.concatenate([q4, zero] if h == 0 else [zero, q4], axis=0)

    for r in range(1, PLANE):
        arrived(st.at[0], c1.at[in_plane(PLANE - r)], s1.at[r - 1], r1.at[r - 1])
    run = jnp.zeros((CHUNK, VROWS), F32)
    for i in range(PLANE):
        run = run * keep_p[i] + c1[i].astype(F32)
    ts[...] = run.astype(BF16)

    def to_later(r):
        return remote(ts, c2.at[z], s2.at[r - 1], r2.at[r - 1], in_line(r))

    def to_near(r):
        @pl.when(lax.div(z + r, far_half) == upper)
        def _():
            to_later(r).start()

    def to_far(r):
        @pl.when(lax.div(z + r, far_half) != upper)
        def _():
            to_later(r).start()

    later_near = far_half - 1 - lax.rem(z, far_half)
    pl.when(later_near > 0)(lambda: pl.semaphore_wait(near_sem, later_near))
    on_later_planes(to_near, range(1, far_half))

    def local_terms(h, half):
        t0, s_rows = half * half_rows, (half + 1) * half_rows
        t = slice(t0, t0 + half_rows)
        y = dot(knat[0:s_rows, :], qs[h, :, t], ((1,), (0,))) + 1.0
        s_index = lax.broadcasted_iota(I32, y.shape, 0)
        t_index = lax.broadcasted_iota(I32, (1, half_rows), 1) + t0
        seen = (s_index <= t_index) & (s_index >= low_row[:, t])
        weight = jnp.where(seen, y * y + 1.0, 0.0).astype(BF16)
        num[h, :, t] = dot(vt[h, :, 0:s_rows], weight, ((1,), (0,)))

    local_terms(0, 0)
    local_terms(0, 1)

    on_earlier_planes(lambda r: arrived(ts, c2.at[z - r], s2.at[r - 1], r2.at[r - 1]))
    run = jnp.zeros((CHUNK, VROWS), F32)
    for i in range(PLANES):
        run = run * jnp.where(i < z, keep_z[i], 1.0) + c2[i].astype(F32)
    for i in range(PLANE):
        rs[i] = run.astype(BF16)
        if i < PLANE - 1:
            run = run * keep_p[i] + c1[i].astype(F32)

    for r in FAR_FIRST:
        to = in_plane(r)
        send(rs.at[to], sin.at[p], s3.at[r - 1], r3.at[r - 1], (z * PLANE + to, mp))
    sin[p] = rs[p]
    pl.when(upper == 0)(lambda: pl.semaphore_wait(far_sem, far_half))
    on_later_planes(to_far)

    local_terms(1, 0)
    local_terms(1, 1)
    ow_load.wait()
    turned = ow[...].T
    ot[...] = turned.reshape(RING, HEADS * VDIM, HEADS * VDIM)

    for r in range(1, PLANE):
        arrived(rs.at[0], sin.at[in_plane(PLANE - r)], s3.at[r - 1], r3.at[r - 1])

    for half in range(2):
        t = slice(half * half_rows, (half + 1) * half_rows)
        for h in range(HEADS):
            part = PLANE // HEADS
            incoming = sin[h * part : (h + 1) * part].reshape(TERMS, VROWS)
            both = num[h, :, t] + dot(incoming, fq[h, :, t], ((0,), (0,)))
            attended = both[0:VDIM, :] * (1.0 / both[VDIM : VDIM + 1, :])
            c = slice(h * VDIM, (h + 1) * VDIM)
            for i in range(2):
                piece = attended[:, i * quarter_rows : (i + 1) * quarter_rows] * gcol[c, :]
                ht[2 * half + i, c, :] = piece.astype(BF16)

    def share(hops, quarter):
        return dot(ot[along_mp(hops)], ht[quarter], ((1,), (0,)))

    def ring(order, i, sign, sbuf, rbuf, ssem, rsem):
        hops, quarter = order[i]
        block = share(sign * hops, quarter)
        if (hops + 1, quarter) in order:
            j = order.index((hops + 1, quarter))
            arrived(sbuf.at[j], rbuf.at[j], ssem.at[j], rsem.at[j])
            block = block + rbuf[j].astype(F32)
        sbuf[i] = block.astype(BF16)
        send(sbuf.at[i], rbuf.at[i], ssem.at[i], rsem.at[i], (seq, along_mp(sign)))

    for i in range(len(RIGHTWARD)):
        ring(RIGHTWARD, i, 1, send_r, recv_r, ssr, rsr)
        ring(LEFTWARD, i, -1, send_l, recv_l, ssl, rsl)
    for quarter in range(QUARTERS):
        own[quarter] = share(0, quarter)
    for quarter in (2, 0, 3, 1):
        i, j = RIGHTWARD.index((1, quarter)), LEFTWARD.index((1, quarter))
        arrived(send_r.at[i], recv_r.at[i], ssr.at[i], rsr.at[i])
        arrived(send_l.at[j], recv_l.at[j], ssl.at[j], rsl.at[j])
        summed = own[quarter] + recv_r[i].astype(F32) + recv_l[j].astype(F32)
        cols = slice(quarter * quarter_rows, (quarter + 1) * quarter_rows)
        out_ref[:, cols] = summed.astype(BF16)

    for copy in sends:
        copy.wait_send()
    on_later_planes(lambda r: to_later(r).wait_send())


def local(tokens, norm_gain, q_weight, k_weight, v_weight, out_gain, o_weight, lengths):
    rows, width = tokens.shape
    wide = HEADS * VDIM
    piece = (wide, rows // QUARTERS)
    dma, vmem = pltpu.SemaphoreType.DMA, pltpu.VMEM
    hbm = pl.BlockSpec(memory_space=pltpu.HBM)
    whole = pl.BlockSpec(memory_space=pltpu.VMEM)
    operands = (
        tokens, norm_gain, q_weight.T, k_weight.T, v_weight.T, out_gain, o_weight, lengths
    )
    turned = pl.pallas_call(
        kernel,
        out_shape=pltpu.VMEM((wide, rows), BF16),
        in_specs=[hbm] * 8,
        out_specs=whole,
        scratch_shapes=[
            pltpu.SMEM(lengths.shape, I32),
            vmem(norm_gain.shape, F32),
            vmem(out_gain.shape, F32),
            vmem((rows, width), BF16),
            vmem((wide + 2 * HEADS * FEAT, width), BF16),
            vmem(o_weight.shape, BF16),
            vmem((RING, wide, wide), BF16),
            vmem((wide, 128), F32),
            vmem((HEADS, VROWS, rows), BF16),
            vmem((HEADS * FEAT, rows), F32),
            vmem((HEADS * FEAT, rows), F32),
            vmem((rows, HEADS * FEAT), BF16),
            vmem((HEADS, HEADS * FEAT, rows), BF16),
            vmem((HEADS, TERMS, rows), BF16),
            vmem((HEADS, TERMS, rows), BF16),
            vmem((HEADS, VROWS, rows), F32),
            vmem((QUARTERS,) + piece, BF16),
            vmem((QUARTERS,) + piece, F32),
            vmem((PLANE, CHUNK, VROWS), BF16),
            vmem((PLANE, CHUNK, VROWS), BF16),
            vmem((CHUNK, VROWS), BF16),
            vmem((PLANES, CHUNK, VROWS), BF16),
            vmem((PLANE, CHUNK, VROWS), BF16),
            vmem((PLANE, CHUNK, VROWS), BF16),
            vmem((len(RIGHTWARD),) + piece, BF16),
            vmem((len(LEFTWARD),) + piece, BF16),
            vmem((len(RIGHTWARD),) + piece, BF16),
            vmem((len(LEFTWARD),) + piece, BF16),
            dma((9,)),
            dma((PLANE - 1,)),
            dma((PLANE - 1,)),
            dma((PLANES - 1,)),
            dma((PLANES - 1,)),
            dma((PLANE - 1,)),
            dma((PLANE - 1,)),
            dma((len(RIGHTWARD),)),
            dma((len(RIGHTWARD),)),
            dma((len(LEFTWARD),)),
            dma((len(LEFTWARD),)),
            pltpu.SemaphoreType.REGULAR,
            pltpu.SemaphoreType.REGULAR,
        ],
        compiler_params=pltpu.CompilerParams(
            collective_id=0, has_side_effects=True, vmem_limit_bytes=40 << 20
        ),
    )(*[pltpu.with_memory_space_constraint(a, pltpu.HBM) for a in operands])
    return turned.T


def solution(mesh):
    placed = (
        P("seq", None),
        P(),
        P(None, "mp"),
        P(None, "mp"),
        P(None, "mp"),
        P("mp"),
        P("mp", None),
        P(),
    )
    return jax.shard_map(
        local, mesh=mesh, in_specs=placed, out_specs=P("seq", "mp"), check_vma=False
    )
```

```python
import functools

import jax
import jax.numpy as jnp
from jax import lax
from jax.experimental import pallas as pl
from jax.experimental.pallas import tpu as pltpu
from jax.sharding import PartitionSpec as P

MESH = pl.DeviceIdType.MESH
F32, BF16, I32 = jnp.float32, jnp.bfloat16, jnp.int32

FEAT = 16
VDIM = 112
HEADS = 2
PLANE = 8
PLANES = 8
RING = 8
TERMS = 192
CHUNK = HEADS * TERMS // PLANE
VROWS = 128

FAR_FIRST = (4, 3, 5, 2, 6, 1, 7)

QUARTERS = 4
RIGHTWARD = ((4, 0), (3, 2), (4, 1), (3, 3), (3, 0), (3, 1)) + tuple(
    (k, q) for k in (2, 1) for q in (2, 3, 0, 1)
)
LEFTWARD = tuple((hops, (quarter + 2) % QUARTERS) for hops, quarter in RIGHTWARD)


def dot(a, b, dims):
    return lax.dot_general(a, b, (dims, ((), ())), preferred_element_type=F32)


def write_features(out, head, u, coefficients, keep):
    square, cross, linear, constant = coefficients
    for d in range(FEAT // 2 + 1):
        turned = u if d == 0 else pltpu.roll(u, d, 0)
        scale = square if d in (0, FEAT // 2) else cross
        rows = u * turned
        if scale != 1.0:
            rows = rows * scale
        if keep is not None:
            rows = rows * keep
        out[head, d * FEAT : (d + 1) * FEAT, :] = rows.astype(BF16)
    base = (FEAT // 2 + 1) * FEAT
    rows = u * linear if linear != 1.0 else u
    if keep is not None:
        rows = rows * keep
    out[head, base : base + FEAT, :] = rows.astype(BF16)
    index = lax.broadcasted_iota(I32, (2 * FEAT, u.shape[1]), 0)
    rows = jnp.where(index == 0, constant, 0.0)
    if keep is not None:
        rows = rows * keep
    out[head, base + FEAT : base + 3 * FEAT, :] = rows.astype(BF16)


def kernel(
    tok_hbm, ng_hbm, wq_hbm, wk_hbm, wv_hbm, og_hbm, ow_hbm, len_hbm,
    out_ref,
    len_ref, ng_ref, og_ref, tok, weights, ow, ot, gcol,
    vt, qt, kt, knat, qs, fk, fq, num, ht, own,
    st, c1, ts, c2, rs, sin, send_r, send_l, recv_r, recv_l,
    load_sem, s1, r1, s2, r2, s3, r3, ssr, rsr, ssl, rsl, near_sem, far_sem,
):
    rows, width = tok.shape
    half_rows, quarter_rows = rows // 2, rows // QUARTERS
    seq, mp = lax.axis_index("seq"), lax.axis_index("mp")
    z, p = lax.div(seq, PLANE), lax.rem(seq, PLANE)
    first_row = seq * rows

    def in_plane(r):
        return lax.rem(p + r, PLANE)

    def along_z(r):
        return lax.rem(z + r, PLANES)

    def along_mp(r):
        return lax.rem(mp + r + RING, RING)

    def in_line(r):
        return ((z + r) * PLANE + p, mp)

    def on_later_planes(act, steps=range(1, PLANES)):
        for r in steps:
            pl.when(z + r < PLANES)(functools.partial(act, r))

    def on_earlier_planes(act):
        for r in range(1, PLANES):
            pl.when(z >= r)(functools.partial(act, r))

    steps = 1
    step_rows = rows // steps
    len_load = pltpu.make_async_copy(len_hbm, len_ref, load_sem.at[6])
    ng_load = pltpu.make_async_copy(ng_hbm, ng_ref, load_sem.at[7])
    og_load = pltpu.make_async_copy(og_hbm, og_ref, load_sem.at[8])
    loads, base = [], 0
    for i, src in enumerate((wv_hbm, wq_hbm, wk_hbm)):
        dst = weights.at[pl.ds(base, src.shape[0]), :]
        loads.append(pltpu.make_async_copy(src, dst, load_sem.at[i]))
        base += src.shape[0]
    tok_loads = [
        pltpu.make_async_copy(
            tok_hbm.at[pl.ds(i * step_rows, step_rows), :],
            tok.at[pl.ds(i * step_rows, step_rows), :],
            load_sem.at[4 + i],
        )
        for i in range(steps)
    ]
    ow_load = pltpu.make_async_copy(ow_hbm, ow, load_sem.at[3])
    for c in [len_load, ng_load, tok_loads[0]] + loads + [og_load]:
        c.start()

    barrier = pltpu.get_barrier_semaphore()
    partners = [(z * PLANE + in_plane(r), mp) for r in range(1, PLANE)]
    partners += [(seq, along_mp(1)), (seq, along_mp(-1))]
    for who in partners:
        pl.semaphore_signal(barrier, inc=1, device_id=who, device_id_type=MESH)
    on_later_planes(
        lambda r: pl.semaphore_signal(barrier, inc=1, device_id=in_line(r), device_id_type=MESH)
    )

    len_load.wait()
    lens = [len_ref[i] for i in range(len_ref.shape[0])]
    ends, total = [], None
    for n in lens:
        total = n if total is None else total + n
        ends.append(total)

    def start_of(position):
        found = 0
        for n, e in zip(lens, ends):
            found = found + jnp.where(e <= position, n, 0)
        return found

    pos_row = first_row + lax.broadcasted_iota(I32, (1, rows), 1)
    starts_row = start_of(pos_row)
    low_row = starts_row - first_row
    last_start = start_of(first_row + rows - 1)
    in_last = jnp.where(pos_row >= last_start, 1.0, 0.0).astype(F32)
    from_before = jnp.where(starts_row < first_row, 1.0, 0.0).astype(F32)

    def kept(row0, count):
        goes_on = start_of(row0 + count - 1) < row0
        return jnp.where(goes_on, 1.0, 0.0).astype(F32)

    plane_rows = PLANE * rows
    keep_p = [kept(z * plane_rows + i * rows, rows) for i in range(PLANE)]
    keep_z = [kept(i * plane_rows, plane_rows) for i in range(PLANES)]

    index = lax.broadcasted_iota(I32, (VROWS - VDIM, rows), 0)
    ones = jnp.where(index == 0, 1.0, 0.0).astype(BF16)
    for h in range(HEADS):
        vt[h, VDIM:VROWS, :] = ones
    for i in range(PLANES):

        @pl.when(i >= z)
        def _():
            c2[i] = jnp.zeros((CHUNK, VROWS), BF16)

    og_load.wait()
    gain_row = og_ref[...].reshape(1, HEADS * VDIM)
    gcol[...] = jnp.broadcast_to(gain_row, (128, HEADS * VDIM)).T

    pl.semaphore_wait(barrier, len(partners) + z)

    far_half = PLANES // 2
    upper = lax.div(z, far_half)

    def say_ready(r):
        same = lax.div(z - r, far_half) == upper

        @pl.when(same)
        def _():
            pl.semaphore_signal(near_sem, inc=1, device_id=in_line(-r), device_id_type=MESH)

        @pl.when(jnp.logical_not(same))
        def _():
            pl.semaphore_signal(far_sem, inc=1, device_id=in_line(-r), device_id_type=MESH)

    on_earlier_planes(say_ready)


    for c in loads:
        c.wait()
    ng_load.wait()
    norm_gain = ng_ref[...].reshape(1, width)
    for i in range(steps):
        tok_loads[i].wait()
        cols = slice(i * step_rows, (i + 1) * step_rows)
        x = tok[cols, :].astype(F32)
        scaled = (x * norm_gain).astype(BF16)
        squares = x * x
        sums = sum(squares[:, j : j + 128] for j in range(0, width, 128))
        row_scale = lax.rsqrt(jnp.sum(sums.T, axis=0, keepdims=True) / width + 1e-06)
        vqk = dot(weights[...], scaled, ((1,), (1,))) * row_scale
        for h in range(HEADS):
            vt[h, 0:VDIM, cols] = vqk[h * VDIM : (h + 1) * VDIM, :].astype(BF16)
        base = HEADS * VDIM
        qt[:, cols] = vqk[base : base + HEADS * FEAT, :]
        k = vqk[base + HEADS * FEAT :, :]
        kt[:, cols] = k
        knat[cols, :] = k.T.astype(BF16)

    ow_load.start()

    masked = in_last.astype(BF16)
    for h in range(HEADS):
        write_features(fk, h, kt[h * FEAT : (h + 1) * FEAT, :], (1.0, 1.0, 1.0, 1.0), None)
        state = dot(fk[h], vt[h] * masked, ((1,), (1,)))
        part = PLANE // HEADS
        st[h * part : (h + 1) * part] = state.astype(BF16).reshape(part, CHUNK, VROWS)

    sends = []

    def remote(src, dst, ssem, rsem, who):
        return pltpu.make_async_remote_copy(
            src_ref=src, dst_ref=dst, send_sem=ssem, recv_sem=rsem,
            device_id=who, device_id_type=MESH,
        )

    def send(src, dst, ssem, rsem, who):
        copy = remote(src, dst, ssem, rsem, who)
        copy.start()
        sends.append(copy)

    def arrived(src, dst, ssem, rsem):
        remote(src, dst, ssem, rsem, (seq, along_mp(1))).wait_recv()

    for r in FAR_FIRST:
        to = in_plane(r)
        send(st.at[to], c1.at[p], s1.at[r - 1], r1.at[r - 1], (z * PLANE + to, mp))
    c1[p] = st[p]

    for h in range(HEADS):
        u = qt[h * FEAT : (h + 1) * FEAT, :]
        write_features(fq, h, u, (1 / 16, 1 / 8, 1 / 2, 2.0), from_before)
        q4 = (u * 0.25).astype(BF16)
        zero = jnp.zeros_like(q4)
        qs[h] = jnp.concatenate([q4, zero] if h == 0 else [zero, q4], axis=0)

    for r in range(1, PLANE):
        arrived(st.at[0], c1.at[in_plane(PLANE - r)], s1.at[r - 1], r1.at[r - 1])
    run = jnp.zeros((CHUNK, VROWS), F32)
    for i in range(PLANE):
        run = run * keep_p[i] + c1[i].astype(F32)
    ts[...] = run.astype(BF16)

    def to_later(r):
        return remote(ts, c2.at[z], s2.at[r - 1], r2.at[r - 1], in_line(r))

    def to_near(r):
        @pl.when(lax.div(z + r, far_half) == upper)
        def _():
            to_later(r).start()

    def to_far(r):
        @pl.when(lax.div(z + r, far_half) != upper)
        def _():
            to_later(r).start()

    later_near = far_half - 1 - lax.rem(z, far_half)
    pl.when(later_near > 0)(lambda: pl.semaphore_wait(near_sem, later_near))
    on_later_planes(to_near, range(1, far_half))

    def local_terms(h, half):
        t0, s_rows = half * half_rows, (half + 1) * half_rows
        t = slice(t0, t0 + half_rows)
        y = dot(knat[0:s_rows, :], qs[h, :, t], ((1,), (0,))) + 1.0
        s_index = lax.broadcasted_iota(I32, y.shape, 0)
        t_index = lax.broadcasted_iota(I32, (1, half_rows), 1) + t0
        seen = (s_index <= t_index) & (s_index >= low_row[:, t])
        weight = jnp.where(seen, y * y + 1.0, 0.0).astype(BF16)
        num[h, :, t] = dot(vt[h, :, 0:s_rows], weight, ((1,), (0,)))

    local_terms(0, 0)
    local_terms(0, 1)

    on_earlier_planes(lambda r: arrived(ts, c2.at[z - r], s2.at[r - 1], r2.at[r - 1]))
    run = jnp.zeros((CHUNK, VROWS), F32)
    for i in range(PLANES):
        run = run * jnp.where(i < z, keep_z[i], 1.0) + c2[i].astype(F32)
    for i in range(PLANE):
        rs[i] = run.astype(BF16)
        if i < PLANE - 1:
            run = run * keep_p[i] + c1[i].astype(F32)

    for r in FAR_FIRST:
        to = in_plane(r)
        send(rs.at[to], sin.at[p], s3.at[r - 1], r3.at[r - 1], (z * PLANE + to, mp))
    sin[p] = rs[p]
    pl.when(upper == 0)(lambda: pl.semaphore_wait(far_sem, far_half))
    on_later_planes(to_far)

    local_terms(1, 0)
    local_terms(1, 1)
    ow_load.wait()
    turned = ow[...].T
    ot[...] = turned.reshape(RING, HEADS * VDIM, HEADS * VDIM)

    for r in range(1, PLANE):
        arrived(rs.at[0], sin.at[in_plane(PLANE - r)], s3.at[r - 1], r3.at[r - 1])

    for half in range(2):
        t = slice(half * half_rows, (half + 1) * half_rows)
        for h in range(HEADS):
            part = PLANE // HEADS
            incoming = sin[h * part : (h + 1) * part].reshape(TERMS, VROWS)
            both = num[h, :, t] + dot(incoming, fq[h, :, t], ((0,), (0,)))
            attended = both[0:VDIM, :] * (1.0 / both[VDIM : VDIM + 1, :])
            c = slice(h * VDIM, (h + 1) * VDIM)
            for i in range(2):
                piece = attended[:, i * quarter_rows : (i + 1) * quarter_rows] * gcol[c, :]
                ht[2 * half + i, c, :] = piece.astype(BF16)

    def share(hops, quarter):
        return dot(ot[along_mp(hops)], ht[quarter], ((1,), (0,)))

    def ring(order, i, sign, sbuf, rbuf, ssem, rsem):
        hops, quarter = order[i]
        block = share(sign * hops, quarter)
        if (hops + 1, quarter) in order:
            j = order.index((hops + 1, quarter))
            arrived(sbuf.at[j], rbuf.at[j], ssem.at[j], rsem.at[j])
            block = block + rbuf[j].astype(F32)
        sbuf[i] = block.astype(BF16)
        send(sbuf.at[i], rbuf.at[i], ssem.at[i], rsem.at[i], (seq, along_mp(sign)))

    for i in range(len(RIGHTWARD)):
        ring(RIGHTWARD, i, 1, send_r, recv_r, ssr, rsr)
        ring(LEFTWARD, i, -1, send_l, recv_l, ssl, rsl)
    for quarter in range(QUARTERS):
        own[quarter] = share(0, quarter)
    for quarter in (2, 0, 3, 1):
        i, j = RIGHTWARD.index((1, quarter)), LEFTWARD.index((1, quarter))
        arrived(send_r.at[i], recv_r.at[i], ssr.at[i], rsr.at[i])
        arrived(send_l.at[j], recv_l.at[j], ssl.at[j], rsl.at[j])
        summed = own[quarter] + recv_r[i].astype(F32) + recv_l[j].astype(F32)
        cols = slice(quarter * quarter_rows, (quarter + 1) * quarter_rows)
        out_ref[:, cols] = summed.astype(BF16)

    for copy in sends:
        copy.wait_send()
    on_later_planes(lambda r: to_later(r).wait_send())


def local(tokens, norm_gain, q_weight, k_weight, v_weight, out_gain, o_weight, lengths):
    rows, width = tokens.shape
    wide = HEADS * VDIM
    piece = (wide, rows // QUARTERS)
    dma, vmem = pltpu.SemaphoreType.DMA, pltpu.VMEM
    hbm = pl.BlockSpec(memory_space=pltpu.HBM)
    whole = pl.BlockSpec(memory_space=pltpu.VMEM)
    operands = (
        tokens, norm_gain, q_weight.T, k_weight.T, v_weight.T, out_gain, o_weight, lengths
    )
    turned = pl.pallas_call(
        kernel,
        out_shape=pltpu.VMEM((wide, rows), BF16),
        in_specs=[hbm] * 8,
        out_specs=whole,
        scratch_shapes=[
            pltpu.SMEM(lengths.shape, I32),
            vmem(norm_gain.shape, F32),
            vmem(out_gain.shape, F32),
            vmem((rows, width), BF16),
            vmem((wide + 2 * HEADS * FEAT, width), BF16),
            vmem(o_weight.shape, BF16),
            vmem((RING, wide, wide), BF16),
            vmem((wide, 128), F32),
            vmem((HEADS, VROWS, rows), BF16),
            vmem((HEADS * FEAT, rows), F32),
            vmem((HEADS * FEAT, rows), F32),
            vmem((rows, HEADS * FEAT), BF16),
            vmem((HEADS, HEADS * FEAT, rows), BF16),
            vmem((HEADS, TERMS, rows), BF16),
            vmem((HEADS, TERMS, rows), BF16),
            vmem((HEADS, VROWS, rows), F32),
            vmem((QUARTERS,) + piece, BF16),
            vmem((QUARTERS,) + piece, F32),
            vmem((PLANE, CHUNK, VROWS), BF16),
            vmem((PLANE, CHUNK, VROWS), BF16),
            vmem((CHUNK, VROWS), BF16),
            vmem((PLANES, CHUNK, VROWS), BF16),
            vmem((PLANE, CHUNK, VROWS), BF16),
            vmem((PLANE, CHUNK, VROWS), BF16),
            vmem((len(RIGHTWARD),) + piece, BF16),
            vmem((len(LEFTWARD),) + piece, BF16),
            vmem((len(RIGHTWARD),) + piece, BF16),
            vmem((len(LEFTWARD),) + piece, BF16),
            dma((9,)),
            dma((PLANE - 1,)),
            dma((PLANE - 1,)),
            dma((PLANES - 1,)),
            dma((PLANES - 1,)),
            dma((PLANE - 1,)),
            dma((PLANE - 1,)),
            dma((len(RIGHTWARD),)),
            dma((len(RIGHTWARD),)),
            dma((len(LEFTWARD),)),
            dma((len(LEFTWARD),)),
            pltpu.SemaphoreType.REGULAR,
            pltpu.SemaphoreType.REGULAR,
        ],
        compiler_params=pltpu.CompilerParams(
            collective_id=0, has_side_effects=True, vmem_limit_bytes=40 << 20
        ),
    )(*[pltpu.with_memory_space_constraint(a, pltpu.HBM) for a in operands])
    return turned.T


def solution(mesh):
    placed = (
        P("seq", None),
        P(),
        P(None, "mp"),
        P(None, "mp"),
        P(None, "mp"),
        P("mp"),
        P("mp", None),
        P(),
    )
    return jax.shard_map(
        local, mesh=mesh, in_specs=placed, out_specs=P("seq", "mp"), check_vma=False
    )
```
